256 devices in a mesh: dp: 16 (over y, z_hi), ctx: 16 (over x, z_lo, core).
Axes of the slice: x: 4, y: 4, z: 8 (z_hi: 4, z_lo: 2; z = z_hi * 2 + z_lo), core: 2. Of those that a mesh axis runs over, the one named last changes fastest.
Arguments:
- route_pos: int32 [16, 2048], P('dp', 'ctx'), may hold values from -1 to 8191, as said below
- x_routed: bfloat16 [16, 2048, 4096], P('dp', 'ctx'), may hold values from -6 to 6
- w_router: bfloat16 [4096], P('dp'), may hold values from -0.09375 to 0.09375
- queries: bfloat16 [16, 2048, 2048], P('dp', 'ctx'), may hold values from -8 to 8
- keys: bfloat16 [16, 2048, 2048], P('dp', 'ctx'), may hold values from -8 to 8
- values: bfloat16 [16, 2048, 2048], P('dp', 'ctx'), may hold values from -6 to 6
- d_gated: float32 [16, 2048, 2048], P('dp', 'ctx'), may hold values from -6 to 6
Outputs:
- grad_queries: float32 [16, 2048, 2048], P('dp', 'ctx')
- grad_keys: float32 [16, 2048, 2048], P('dp', 'ctx')
- grad_values: float32 [16, 2048, 2048], P('dp', 'ctx')
- router_grad: float32 [4096], P('dp')
The draws below stay inside these ranges and needn't reach their ends.
Inputs may be any that keep to these rules, and one draw needn't show every extreme that they name: `route_pos`: in each sequence, context shard c lists in its 128 slots the increasing positions of its routed tokens, all from c * 512 to (c + 1) * 512 - 1, then -1 in its unused slots. A shard holds 0 to 128 routed tokens and a sequence 1024 in all; in every sequence some shard holds exactly 128 and some shard none.
All inputs are finite; a program needn't handle non-finite values.
Results may differ from the reference program's by a relative error of at most 0.017.
Values may be sent and summed in bfloat16 or wider, within the bound.
A program may use at most 128 MiB of HBM per device.

```python
from functools import partial
import jax
import jax.numpy as jnp
from jax import lax

D = 4096
HEAD = 128
HEADS = 16
TOK_DEV = 512
CAP = 128
ROUTED = 1024
SLOTS = 2048
SEQS = 16
HD = 2048


def shard_positions(shard_key, count, index):
    slot_index = jnp.arange(CAP, dtype=jnp.int32)
    shuffled = jax.random.permutation(shard_key, jnp.arange(TOK_DEV, dtype=jnp.int32))[:CAP]
    chosen = jnp.sort(jnp.where(slot_index < count, shuffled, TOK_DEV + 1))
    return jnp.where(slot_index < count, chosen + index * TOK_DEV, -1).astype(jnp.int32)


def sequence_positions(seq_key):
    shards = SLOTS // CAP
    pair_count = shards // 2
    half_cap = CAP // 2
    key_order, key_moves, key_rows = jax.random.split(seq_key, 3)
    move_sizes = jax.random.randint(key_moves, (pair_count,), 0, half_cap).astype(jnp.int32)
    move_sizes = move_sizes.at[0].set(half_cap)
    shuffle_order = jax.random.permutation(key_order, jnp.arange(shards, dtype=jnp.int32))
    shifted = jnp.zeros((shards,), jnp.int32).at[shuffle_order[:pair_count]].set(move_sizes)
    shifted = shifted.at[shuffle_order[pair_count:]].set(-move_sizes)
    counts = half_cap + shifted
    shard_keys = jax.random.split(key_rows, shards)
    position_table = jax.vmap(shard_positions)(shard_keys, counts, jnp.arange(shards, dtype=jnp.int32))
    return position_table.reshape(SLOTS)


def draw_route_pos(key, part):
    seq_keys = jax.random.split(jax.random.fold_in(key, 11), SEQS)
    return jax.vmap(sequence_positions)(seq_keys).astype(jnp.int32)


def query_key_pair(key):
    base_key = jax.random.fold_in(key, 29)
    key_query, key_key = jax.random.split(base_key, 2)
    full_shape = (SEQS, SLOTS, HEADS * HEAD)
    query_draw = jnp.clip(jax.random.normal(key_query, full_shape, jnp.float32), -6.0, 6.0)
    key_draw = jnp.clip(jax.random.normal(key_key, full_shape, jnp.float32), -6.0, 6.0)
    return (query_draw, key_draw)


def draw_queries(key, part):
    return query_key_pair(key)[0].astype(jnp.bfloat16)


def draw_keys(key, part):
    return query_key_pair(key)[1].astype(jnp.bfloat16)


def block_levels(rng, shape, cuts, least, top_value):
    def one(axis_at, shards_of):
        heights = jax.random.uniform(jax.random.fold_in(jax.random.fold_in(rng, 6), axis_at), (shards_of,), jnp.float32, least / len(cuts), top_value / len(cuts))
        return jnp.repeat(jnp.exp(heights), shape[axis_at] // shards_of).reshape((-1,) + (1,) * (len(shape) - axis_at - 1))

    factor_of = one(*cuts[0])
    for cut in cuts[1:]:
        factor_of = factor_of * one(*cut)
    return factor_of


def centred(own_key, dims, width, limit, pieces=(), kind=jnp.bfloat16):
    array = jax.random.normal(own_key, dims, jnp.float32) * width
    if len(pieces) > 0:
        array = block_levels(own_key, dims, pieces, -0.22, 0.18) * array
    return jnp.clip(array, min=-limit, max=limit).astype(kind)


def setup_inputs(seed: int = 0) -> dict:
    key_of = jax.random.split(jax.random.key(seed), 8)
    route_pos = draw_route_pos(jax.random.fold_in(key_of[7], 71), 0)
    x_routed = centred(key_of[1], (SEQS, SLOTS, D), 1.0, 6.0, ((0, 16), (1, 16)))
    w_router = centred(key_of[2], (D,), D ** -0.5, 0.09375, ((0, 16),))
    queries = draw_queries(jax.random.fold_in(key_of[7], 71), 0)
    keys = draw_keys(jax.random.fold_in(key_of[7], 71), 0)
    values = centred(key_of[5], (SEQS, SLOTS, HD), 1.0, 6.0, ((0, 16), (1, 16)))
    d_gated = centred(key_of[6], (SEQS, SLOTS, HD), 1.0, 6.0, ((0, 16), (1, 16)), jnp.float32)
    return {"route_pos": route_pos, "x_routed": x_routed, "w_router": w_router, "queries": queries, "keys": keys, "values": values, "d_gated": d_gated}


NEG_FILL = -1e30


def head_backward(allowed, score_scale, operands):
    query_head, key_head, value_head, grad_head = operands
    scores = jnp.dot(query_head, key_head.T, preferred_element_type=jnp.float32) * score_scale
    scores = jnp.where(allowed, scores, NEG_FILL)
    row_max = jnp.max(scores, axis=-1, keepdims=True)
    exponent = jnp.exp(scores - row_max)
    row_total = jnp.sum(exponent, axis=-1, keepdims=True)
    weights = exponent / row_total
    weights_low = weights.astype(jnp.bfloat16)
    attended = jnp.dot(weights_low, value_head, preferred_element_type=jnp.float32)
    grad_weights = jnp.dot(grad_head, value_head.T, preferred_element_type=jnp.float32)
    row_delta = jnp.sum(grad_head.astype(jnp.float32) * attended, axis=-1, keepdims=True)
    grad_scores = weights * (grad_weights - row_delta) * score_scale
    grad_low = grad_scores.astype(jnp.bfloat16)
    grad_query = jnp.dot(grad_low, key_head, preferred_element_type=jnp.float32)
    shards = query_head.shape[0] // CAP
    score_blocks = grad_low.astype(jnp.float32).reshape(shards, CAP, -1)
    weight_blocks = weights_low.astype(jnp.float32).reshape(shards, CAP, -1)
    query_blocks = query_head.astype(jnp.float32).reshape(shards, CAP, -1)
    grad_blocks = grad_head.astype(jnp.float32).reshape(shards, CAP, -1)
    key_terms = jnp.einsum('nqk,nqd->nkd', score_blocks, query_blocks)
    value_terms = jnp.einsum('nqk,nqd->nkd', weight_blocks, grad_blocks)
    key_terms = lax.optimization_barrier(key_terms.astype(jnp.bfloat16)).astype(jnp.float32)
    value_terms = lax.optimization_barrier(value_terms.astype(jnp.bfloat16)).astype(jnp.float32)
    return attended, grad_query, jnp.sum(key_terms, axis=0), jnp.sum(value_terms, axis=0)


def split_heads(rows_in):
    return rows_in.reshape(SLOTS, HEADS, HEAD).transpose(1, 0, 2)


def join_heads(per_head):
    return per_head.transpose(1, 0, 2).reshape(SLOTS, HEADS * HEAD)


def one_sequence(w_router, operands):
    positions, x_rows, query_rows, key_rows, value_rows, grad_rows = operands
    is_live = positions >= 0
    live_float = is_live.astype(jnp.float32)
    router_logit = jnp.dot(x_rows, w_router, preferred_element_type=jnp.float32)
    gate_value = jax.nn.sigmoid(router_logit)
    grad_out = ((gate_value * live_float)[:, None] * grad_rows).astype(jnp.bfloat16)
    allowed = is_live[:, None] & is_live[None, :] & (positions[None, :] <= positions[:, None])
    attended, grad_query, grad_key, grad_value = lax.map(
        partial(head_backward, allowed, HEAD ** -0.5),
        (split_heads(query_rows), split_heads(key_rows), split_heads(value_rows), split_heads(grad_out)))
    attended = join_heads(attended)
    grad_gate = jnp.sum(attended * grad_rows, axis=-1) * live_float
    grad_logit = grad_gate * gate_value * (1.0 - gate_value)
    router_term = jnp.dot(grad_logit, x_rows.astype(jnp.float32), precision=lax.Precision.HIGHEST)
    return join_heads(grad_query), join_heads(grad_key), join_heads(grad_value), router_term


def reference(route_pos, x_routed, w_router, queries, keys, values, d_gated):
    grad_queries, grad_keys, grad_values, router_terms = lax.map(
        partial(one_sequence, w_router), (route_pos, x_routed, queries, keys, values, d_gated))
    router_grad = jnp.sum(router_terms, axis=0) / float(SEQS * ROUTED)
    return grad_queries, grad_keys, grad_values, router_grad
```

```python
import functools

import jax
import jax.numpy as jnp
from jax import lax
from jax.experimental import pallas as pl
from jax.experimental.pallas import tpu as pltpu
from jax.sharding import PartitionSpec as P

HEAD = 128
NEG_FILL = -1e30
LOG2E = 1.4426950408889634
MESH = pl.DeviceIdType.MESH
F32 = jnp.float32
BF16 = jnp.bfloat16
PAIR = 2
NT = (((1,), (1,)), ((), ()))
CH_K, CH_Q, CH_V, CH_D, CH_BIAS, CH_W, CH_GATE, CH_DELTA, CH_TERM, CH_SUM, CH_GQ, CH_GK, CH_GV = range(13)


def kernel(
    n_ctx,
    n_dp,
    total_routed,
    pos_ref,
    w_ref,
    x_hbm,
    q_hbm,
    k_hbm,
    v_hbm,
    d_hbm,
    gq_ref,
    gk_ref,
    gv_ref,
    rg_ref,
    x_v,
    d_v,
    d_send,
    k_all,
    q_all,
    v_all,
    d_all,
    bias_all,
    bias_own,
    w_all,
    w_own,
    gate_all,
    gate_own,
    bias_col,
    kt_all,
    vt_all,
    s_buf,
    e_buf,
    l_buf,
    att_buf,
    ds_t,
    ds_n,
    delta_buf,
    delta_send,
    delta_all,
    dqt,
    gq_send,
    gk_send,
    gv_send,
    term_send,
    term_all,
    sum_send,
    sum_all,
    local_sem,
    send_sem,
    recv_sem,
):
    me = lax.axis_index("ctx")
    me_dp = lax.axis_index("dp")
    rows = q_hbm.shape[0]
    block = PAIR * rows
    blocks = n_ctx // PAIR
    scale = HEAD ** (-0.5)
    chunk = w_ref.shape[1]

    barrier = pltpu.get_barrier_semaphore()
    for o in range(1, n_ctx):
        pl.semaphore_signal(barrier, inc=1, device_id={"ctx": lax.rem(me + o, n_ctx)}, device_id_type=MESH)
    for o in range(1, n_dp):
        pl.semaphore_signal(barrier, inc=1, device_id={"dp": lax.rem(me_dp + o, n_dp)}, device_id_type=MESH)

    def cols(ref, at):
        return ref.at[:, pl.ds(pl.multiple_of(at * HEAD, HEAD), HEAD)]

    local = [
        pltpu.make_async_copy(d_hbm, d_v, local_sem.at[0]),
        pltpu.make_async_copy(x_hbm, x_v, local_sem.at[1]),
        pltpu.make_async_copy(cols(k_hbm, me), k_all.at[me], local_sem.at[2]),
        pltpu.make_async_copy(cols(q_hbm, me), q_all.at[me], local_sem.at[3]),
        pltpu.make_async_copy(cols(v_hbm, me), v_all.at[me], local_sem.at[4]),
    ]
    for copy in local:
        copy.start()

    def remote(src, dst, channel, axis, peer):
        return pltpu.make_async_remote_copy(
            src_ref=src,
            dst_ref=dst,
            send_sem=send_sem.at[channel],
            recv_sem=recv_sem.at[channel],
            device_id={axis: peer},
            device_id_type=MESH,
        )

    def to_peers(source_of, dst, channel, axis, n, mine):
        for o in range(1, n):
            peer = lax.rem(mine + o, n)
            remote(source_of(peer), dst, channel, axis, peer).start()

    def arrived(ref, channel):
        remote(ref, ref, channel, "ctx", lax.rem(me + 1, n_ctx)).wait_recv()

    def sent(ref, channel):
        remote(ref, ref, channel, "ctx", lax.rem(me + 1, n_ctx)).wait_send()

    live = pos_ref[...] >= 0
    bias_row = jnp.broadcast_to(jnp.where(live, 0.0, NEG_FILL).astype(F32), bias_own.shape)
    bias_own[...] = bias_row
    bias_all[me] = bias_row
    w_rows = jnp.broadcast_to(w_ref[...].astype(F32), w_own.shape).astype(BF16)
    w_own[...] = w_rows
    w_all[me_dp] = w_rows
    local[0].wait()
    for h in range(n_ctx):
        d_send[h] = d_v[:, h * HEAD : (h + 1) * HEAD].astype(BF16)
    d_all[me] = d_send[me]

    pl.semaphore_wait(barrier, n_ctx + n_dp - 2)

    to_peers(lambda p: w_own, w_all.at[me_dp], CH_W, "dp", n_dp, me_dp)
    to_peers(lambda p: bias_own, bias_all.at[me], CH_BIAS, "ctx", n_ctx, me)
    to_peers(lambda p: cols(k_hbm, p), k_all.at[me], CH_K, "ctx", n_ctx, me)
    to_peers(lambda p: cols(q_hbm, p), q_all.at[me], CH_Q, "ctx", n_ctx, me)
    to_peers(lambda p: cols(v_hbm, p), v_all.at[me], CH_V, "ctx", n_ctx, me)
    to_peers(lambda p: d_send.at[p], d_all.at[me], CH_D, "ctx", n_ctx, me)

    few = pl.ds(0, n_ctx - 1)
    few_dp = pl.ds(0, n_dp - 1)

    local[1].wait()
    if n_dp > 1:
        arrived(w_all.at[few_dp], CH_W)
    logit = jnp.zeros((16, rows), F32)
    for p in range(n_dp):
        logit += lax.dot_general(w_all[p], x_v[:, p * chunk : (p + 1) * chunk], NT, preferred_element_type=F32)
    gate = jax.nn.sigmoid(logit[0:8])
    gate_live = jnp.where(jnp.broadcast_to(live, gate.shape), gate, 0.0)
    gate_own[...] = gate_live
    gate_all[me] = gate_live

    arrived(bias_all.at[few], CH_BIAS)
    for s in range(n_ctx):
        bias_col[s] = jnp.broadcast_to(bias_all[s][0:1], (HEAD, rows)).T
    to_peers(lambda p: gate_own, gate_all.at[me], CH_GATE, "ctx", n_ctx, me)

    local[2].wait()
    arrived(k_all.at[few], CH_K)

    def pair(ref, at):
        return ref[pl.ds(at * PAIR, PAIR)].reshape(block, HEAD)

    def transposed(src, dst):
        def step(b, carry):
            dst[b] = pair(src, b).T
            return carry

        lax.fori_loop(0, blocks, step, 0)

    transposed(k_all, kt_all)
    local[3].wait()
    arrived(q_all.at[few], CH_Q)

    key_at = lax.broadcasted_iota(jnp.int32, (block, block), 0)
    query_at = lax.broadcasted_iota(jnp.int32, (block, block), 1)
    causal = key_at <= query_at

    def score_block(i, carry):
        q_i = pair(q_all, i)

        def scores(j):
            s = lax.dot_general(pair(k_all, j), q_i, NT, preferred_element_type=F32)
            b = bias_col[pl.ds(j * PAIR, PAIR)].reshape(block, rows)
            return s + jnp.concatenate([b] * PAIR, axis=1)

        def first(j, top):
            s = scores(j)
            s_buf[j] = s
            return jnp.maximum(top, jnp.max(s, axis=0, keepdims=True))

        s_diag = jnp.where(causal, scores(i), NEG_FILL)
        s_buf[i] = s_diag
        top = lax.fori_loop(0, i, first, jnp.max(s_diag, axis=0, keepdims=True))

        def second(j, total):
            e = jnp.exp2((s_buf[j] - top) * (scale * LOG2E))
            e_buf[j, i] = e.astype(BF16)
            return total + jnp.sum(e, axis=0, keepdims=True)

        l_buf[i] = lax.fori_loop(0, i + 1, second, jnp.zeros((1, block), F32))
        return carry

    lax.fori_loop(0, blocks, score_block, 0)

    local[4].wait()
    arrived(v_all.at[few], CH_V)
    transposed(v_all, vt_all)

    def attend_block(i, carry):
        def step(j, acc):
            return acc + jnp.dot(vt_all[j], e_buf[j, i], preferred_element_type=F32)

        att_buf[i] = lax.fori_loop(0, i + 1, step, jnp.zeros((HEAD, block), F32))
        return carry

    lax.fori_loop(0, blocks, attend_block, 0)

    arrived(gate_all.at[few], CH_GATE)
    arrived(d_all.at[few], CH_D)

    def delta_block(i, carry):
        gates = jnp.concatenate([gate_all[i * PAIR + s][0:1] for s in range(PAIR)], axis=1)
        inverse = 1.0 / l_buf[i]
        scaled = (pair(d_all, i).astype(F32).T * (gates * inverse)).astype(BF16)
        ds_t[i] = scaled
        ds_n[i] = scaled.astype(F32).T.astype(BF16)
        delta = jnp.sum(scaled.astype(F32) * att_buf[i], axis=0, keepdims=True)
        delta_buf[i] = delta * inverse
        for s in range(PAIR):
            delta_send[i * PAIR + s] = jnp.broadcast_to(delta[:, s * rows : (s + 1) * rows], (8, rows))
        dqt[i] = jnp.zeros((HEAD, block), F32)
        return carry

    lax.fori_loop(0, blocks, delta_block, 0)
    delta_all[me] = delta_send[me]
    to_peers(lambda p: delta_send.at[p], delta_all.at[me], CH_DELTA, "ctx", n_ctx, me)

    home = me // PAIR

    def send_back(send, out, channel, b):
        for s in range(PAIR):
            peer = b * PAIR + s

            @pl.when(peer != me)
            def _():
                remote(send.at[peer], cols(out, me), channel, "ctx", peer).start()

    def key_block(step, carry):
        j = lax.rem(home + step, blocks)
        v_j = pair(v_all, j)

        def inner(i, acc):
            dk, dv = acc
            e = e_buf[j, i]
            dw = jnp.dot(v_j, ds_t[i], preferred_element_type=F32)
            g = (e.astype(F32) * (dw - delta_buf[i])).astype(BF16)
            dk += jnp.dot(g, pair(q_all, i), preferred_element_type=F32)
            dv += jnp.dot(e, ds_n[i], preferred_element_type=F32)
            dqt[i] += jnp.dot(kt_all[j], g, preferred_element_type=F32)
            return dk, dv

        zero = jnp.zeros((block, HEAD), F32)
        dk, dv = lax.fori_loop(j, blocks, inner, (zero, zero))
        gk_send[pl.ds(j * PAIR, PAIR)] = (dk * scale).astype(BF16).reshape(PAIR, rows, HEAD)
        gv_send[pl.ds(j * PAIR, PAIR)] = dv.astype(BF16).reshape(PAIR, rows, HEAD)

        @pl.when(step > 0)
        def _():
            before = lax.rem(home + step + blocks - 1, blocks)
            send_back(gk_send, gk_ref, CH_GK, before)
            send_back(gv_send, gv_ref, CH_GV, before)

        return carry

    lax.fori_loop(0, blocks, key_block, 0)
    last = lax.rem(home + blocks - 1, blocks)
    send_back(gk_send, gk_ref, CH_GK, last)
    send_back(gv_send, gv_ref, CH_GV, last)

    def query_out(b, carry):
        gq_send[pl.ds(b * PAIR, PAIR)] = (dqt[b] * scale).T.astype(BF16).reshape(PAIR, rows, HEAD)
        return carry

    lax.fori_loop(0, blocks, query_out, 0)
    to_peers(lambda p: gq_send.at[p], cols(gq_ref, me), CH_GQ, "ctx", n_ctx, me)
    own = [
        pltpu.make_async_copy(gq_send.at[me], cols(gq_ref, me), local_sem.at[5]),
        pltpu.make_async_copy(gk_send.at[me], cols(gk_ref, me), local_sem.at[6]),
        pltpu.make_async_copy(gv_send.at[me], cols(gv_ref, me), local_sem.at[7]),
    ]
    for copy in own:
        copy.start()

    arrived(delta_all.at[few], CH_DELTA)
    row_sum = delta_all[0]
    for h in range(1, n_ctx):
        row_sum += delta_all[h]
    grad_logit = row_sum * (1.0 - gate)
    high = grad_logit.astype(BF16)
    rest = grad_logit - high.astype(F32)
    middle = rest.astype(BF16)
    low = (rest - middle.astype(F32)).astype(BF16)
    which = lax.broadcasted_iota(jnp.int32, (8, rows), 0)
    split = jnp.where(which == 0, high.astype(F32), jnp.where(which == 1, middle.astype(F32), low.astype(F32)))
    split = jnp.where(which < 3, split, 0.0).astype(BF16)
    for p in range(n_dp):
        term_send[p] = jnp.dot(split, x_v[:, p * chunk : (p + 1) * chunk], preferred_element_type=F32)
    term_all[me_dp] = term_send[me_dp]
    to_peers(lambda p: term_send.at[p], term_all.at[me_dp], CH_TERM, "dp", n_dp, me_dp)
    if n_dp > 1:
        arrived(term_all.at[few_dp], CH_TERM)
    term_sum = term_all[0]
    for p in range(1, n_dp):
        term_sum += term_all[p]
    term_sum = jnp.broadcast_to(jnp.sum(term_sum, axis=0, keepdims=True), sum_send.shape)
    sum_send[...] = term_sum
    sum_all[me] = term_sum
    to_peers(lambda p: sum_send, sum_all.at[me], CH_SUM, "ctx", n_ctx, me)
    arrived(sum_all.at[few], CH_SUM)
    everything = sum_all[0]
    for c in range(1, n_ctx):
        everything += sum_all[c]
    rg_ref[...] = everything * (1.0 / total_routed)

    most = pl.ds(0, (n_ctx - 1) * HEAD)
    arrived(gk_ref.at[:, most], CH_GK)
    arrived(gv_ref.at[:, most], CH_GV)
    arrived(gq_ref.at[:, most], CH_GQ)
    for copy in own:
        copy.wait()
    for ref, channel in (
        (k_all, CH_K),
        (q_all, CH_Q),
        (v_all, CH_V),
        (d_all, CH_D),
        (bias_all, CH_BIAS),
        (gate_all, CH_GATE),
        (delta_all, CH_DELTA),
        (sum_all, CH_SUM),
        (gq_send, CH_GQ),
        (gk_send, CH_GK),
        (gv_send, CH_GV),
    ):
        sent(ref.at[few], channel)
    if n_dp > 1:
        sent(w_all.at[few_dp], CH_W)
        sent(term_all.at[few_dp], CH_TERM)


def body(route_pos, x_routed, w_router, queries, keys, values, d_gated):
    n_ctx = lax.axis_size("ctx")
    n_dp = lax.axis_size("dp")
    rows, width = queries.shape[1:]
    blocks = n_ctx // PAIR
    block = PAIR * rows
    total_routed = float(n_dp * n_ctx * rows // 2)
    chunk = w_router.shape[0]
    vmem = pl.BlockSpec(memory_space=pltpu.VMEM)
    anywhere = pl.BlockSpec(memory_space=pl.ANY)
    heads = pltpu.VMEM((n_ctx, rows, HEAD), BF16)
    small = pltpu.VMEM((n_ctx, 8, rows), F32)
    small_own = pltpu.VMEM((8, rows), F32)
    out = jax.ShapeDtypeStruct((rows, width), BF16)
    gq, gk, gv, rg = pl.pallas_call(
        functools.partial(kernel, n_ctx, n_dp, total_routed),
        out_shape=(out, out, out, jax.ShapeDtypeStruct((8, chunk), F32)),
        in_specs=[vmem, vmem] + [anywhere] * 5,
        out_specs=(anywhere, anywhere, anywhere, vmem),
        scratch_shapes=[
            pltpu.VMEM(x_routed.shape[1:], BF16),
            pltpu.VMEM((rows, width), F32),
            heads,
            heads,
            heads,
            heads,
            heads,
            small,
            small_own,
            pltpu.VMEM((n_dp, 16, chunk), BF16),
            pltpu.VMEM((16, chunk), BF16),
            small,
            small_own,
            pltpu.VMEM((n_ctx, rows, rows), F32),
            pltpu.VMEM((blocks, HEAD, block), BF16),
            pltpu.VMEM((blocks, HEAD, block), BF16),
            pltpu.VMEM((blocks, block, block), F32),
            pltpu.VMEM((blocks, blocks, block, block), BF16),
            pltpu.VMEM((blocks, 1, block), F32),
            pltpu.VMEM((blocks, HEAD, block), F32),
            pltpu.VMEM((blocks, HEAD, block), BF16),
            pltpu.VMEM((blocks, block, HEAD), BF16),
            pltpu.VMEM((blocks, 1, block), F32),
            small,
            small,
            pltpu.VMEM((blocks, HEAD, block), F32),
            heads,
            heads,
            heads,
            pltpu.VMEM((n_dp, 8, chunk), F32),
            pltpu.VMEM((n_dp, 8, chunk), F32),
            pltpu.VMEM((8, chunk), F32),
            pltpu.VMEM((n_ctx, 8, chunk), F32),
            pltpu.SemaphoreType.DMA((8,)),
            pltpu.SemaphoreType.DMA((13,)),
            pltpu.SemaphoreType.DMA((13,)),
        ],
        compiler_params=pltpu.CompilerParams(collective_id=0, has_side_effects=True, vmem_limit_bytes=56 * 1024 * 1024),
        name="routed_backward",
    )(route_pos, w_router[None], x_routed[0], queries[0], keys[0], values[0], d_gated[0])
    return (gq.astype(F32)[None], gk.astype(F32)[None], gv.astype(F32)[None], rg[0])


def solution(mesh):
    placed = (
        P("dp", "ctx"),
        P("dp", "ctx", None),
        P("dp"),
        P("dp", "ctx", None),
        P("dp", "ctx", None),
        P("dp", "ctx", None),
        P("dp", "ctx", None),
    )
    return jax.shard_map(
        body,
        mesh=mesh,
        in_specs=placed,
        out_specs=(P("dp", "ctx", None), P("dp", "ctx", None), P("dp", "ctx", None), P("dp")),
        check_vma=False,
    )
```

```python
import functools

import jax
import jax.numpy as jnp
from jax import lax
from jax.experimental import pallas as pl
from jax.experimental.pallas import tpu as pltpu
from jax.sharding import PartitionSpec as P

HEAD = 128
NEG_FILL = -1e30
LOG2E = 1.4426950408889634
MESH = pl.DeviceIdType.MESH
F32 = jnp.float32
BF16 = jnp.bfloat16
BLOCK = 256
NT = (((1,), (1,)), ((), ()))
CH_K, CH_Q, CH_V, CH_D, CH_LIVE, CH_W_Z, CH_W_Y, CH_DELTA, CH_TERM_Y, CH_TERM_Z, CH_SUM, CH_GQ, CH_GK, CH_GV = range(14)
CHANNELS = 14


def dot(a, b):
    return jnp.dot(a, b, preferred_element_type=F32)


def dot_nt(a, b):
    return lax.dot_general(a, b, NT, preferred_element_type=F32)


def three_rows(row):
    high = row.astype(BF16).astype(F32)
    middle = (row - high).astype(BF16).astype(F32)
    low = row - high - middle
    which = lax.broadcasted_iota(jnp.int32, row.shape, 0)
    split = jnp.where(which == 0, high, jnp.where(which == 1, middle, low))
    return jnp.where(which < 3, split, 0.0).astype(BF16)


def kernel(
    n_ctx,
    n_y,
    n_z,
    pos_ref,
    w_ref,
    x_hbm,
    q_hbm,
    k_hbm,
    v_hbm,
    d_hbm,
    gq_ref,
    gk_ref,
    gv_ref,
    rg_ref,
    x_v,
    d_v,
    d_send,
    kq_all,
    v_all,
    d_all,
    live_all,
    live_own,
    w_all,
    rank_row,
    pick,
    place,
    kq_c,
    kt_c,
    v_c,
    d_c,
    p_buf,
    ds_buf,
    gkq_c,
    gv_c,
    delta_send,
    delta_all,
    gq_send,
    gk_send,
    gv_send,
    term_send,
    term_y,
    term_half,
    term_z,
    sum_send,
    sum_all,
    local_sem,
    send_sem,
    recv_sem,
):
    me = lax.axis_index("ctx")
    me_dp = lax.axis_index("dp")
    n_dp = n_y * n_z
    me_y, me_z = me_dp // n_z, lax.rem(me_dp, n_z)
    rows = q_hbm.shape[0]
    slots = n_ctx * rows
    routed = slots // 2
    blocks = routed // BLOCK
    per_block = BLOCK // rows
    scale = HEAD ** (-0.5)
    chunk = w_all.shape[2]
    total_routed = float(n_dp * routed)

    def z_peer(o):
        return me_y * n_z + lax.rem(me_z + o, n_z)

    def y_peer(o):
        return lax.rem(me_y + o, n_y) * n_z + me_z

    barrier = pltpu.get_barrier_semaphore()
    for o in range(1, n_z):
        pl.semaphore_signal(barrier, inc=1, device_id={"dp": z_peer(o)}, device_id_type=MESH)
    for o in range(1, n_y):
        pl.semaphore_signal(barrier, inc=1, device_id={"dp": y_peer(o)}, device_id_type=MESH)
    for o in range(1, n_ctx):
        pl.semaphore_signal(barrier, inc=1, device_id={"ctx": lax.rem(me + o, n_ctx)}, device_id_type=MESH)

    def cols(ref, at):
        return ref.at[:, pl.ds(pl.multiple_of(at * HEAD, HEAD), HEAD)]

    local = [
        pltpu.make_async_copy(d_hbm, d_v, local_sem.at[0]),
        pltpu.make_async_copy(x_hbm, x_v, local_sem.at[1]),
        pltpu.make_async_copy(cols(k_hbm, me), kq_all.at[me, :, pl.ds(0, HEAD)], local_sem.at[2]),
        pltpu.make_async_copy(cols(q_hbm, me), kq_all.at[me, :, pl.ds(HEAD, HEAD)], local_sem.at[3]),
        pltpu.make_async_copy(cols(v_hbm, me), v_all.at[me], local_sem.at[4]),
    ]
    for copy in local:
        copy.start()

    def remote(src, dst, channel, axis, peer):
        return pltpu.make_async_remote_copy(
            src_ref=src,
            dst_ref=dst,
            send_sem=send_sem.at[channel],
            recv_sem=recv_sem.at[channel],
            device_id={axis: peer},
            device_id_type=MESH,
        )

    def to_peers(source_of, dst, channel, axis, n, mine):
        for o in range(1, n):
            peer = lax.rem(mine + o, n)
            remote(source_of(peer), dst, channel, axis, peer).start()

    def arrived(ref, channel):
        remote(ref, ref, channel, "ctx", lax.rem(me + 1, n_ctx)).wait_recv()

    def sent(ref, channel):
        remote(ref, ref, channel, "ctx", lax.rem(me + 1, n_ctx)).wait_send()

    few = pl.ds(0, n_ctx - 1)

    live_row = jnp.where(jnp.broadcast_to(pos_ref[...], (8, rows)) >= 0, 1.0, 0.0).astype(F32)
    live_own[...] = live_row[0:1]
    live_all[me] = live_row[0:1]
    w_all[me_dp] = w_ref[...].reshape(1, chunk)

    pl.semaphore_wait(barrier, n_ctx + n_y + n_z - 3)

    for o in range(1, n_z):
        remote(w_all.at[me_dp], w_all.at[me_dp], CH_W_Z, "dp", z_peer(o)).start()
    to_peers(lambda p: live_own, live_all.at[me], CH_LIVE, "ctx", n_ctx, me)
    to_peers(lambda p: cols(k_hbm, p), kq_all.at[me, :, pl.ds(0, HEAD)], CH_K, "ctx", n_ctx, me)
    to_peers(lambda p: cols(q_hbm, p), kq_all.at[me, :, pl.ds(HEAD, HEAD)], CH_Q, "ctx", n_ctx, me)
    to_peers(lambda p: cols(v_hbm, p), v_all.at[me], CH_V, "ctx", n_ctx, me)

    local[1].wait()
    if n_z > 1:
        arrived(w_all.at[pl.ds(0, n_z - 1)], CH_W_Z)
    own_y = pl.ds(me_y * n_z, n_z)
    for o in range(1, n_y):
        remote(w_all.at[own_y], w_all.at[own_y], CH_W_Y, "dp", y_peer(o)).start()
    if n_y > 1:
        arrived(w_all.at[pl.ds(0, (n_y - 1) * n_z)], CH_W_Y)
    logit = jnp.zeros((rows, rows), F32)
    for p in range(n_dp):
        w_p = jnp.broadcast_to(w_all[p].astype(F32), (rows, chunk)).astype(BF16)
        logit += dot_nt(x_v[:, p * chunk : (p + 1) * chunk], w_p)
    gate = jax.nn.sigmoid(logit)
    gate_row = gate.T[0:8]
    factor = gate * jnp.broadcast_to(live_row[0:1], (rows, rows)).T
    local[0].wait()
    for h in range(n_ctx):
        d_send[h] = (d_v[:, h * HEAD : (h + 1) * HEAD] * factor).astype(BF16)
    d_all[me] = d_send[me]

    arrived(live_all.at[few], CH_LIVE)
    lane = lax.broadcasted_iota(jnp.int32, (8, rows), 1).astype(F32)
    before = jnp.zeros((8, rows), F32)
    for s in range(n_ctx):
        live_s = jnp.broadcast_to(live_all[s], (8, rows))
        rank_row[s] = jnp.where(live_s > 0.0, before + lane, -1.0)
        before = before + jnp.sum(live_s, axis=1, keepdims=True)

    to_peers(lambda p: d_send.at[p], d_all.at[me], CH_D, "ctx", n_ctx, me)

    token_row = lax.broadcasted_iota(jnp.int32, (BLOCK, rows), 0).astype(F32)
    token_lane = lax.broadcasted_iota(jnp.int32, (rows, routed), 1).astype(F32)

    def slots_of(b):
        first = b * per_block
        return first, min(n_ctx, first + (routed + BLOCK) // rows)

    for b in range(blocks):
        first, last = slots_of(b)
        for s in range(first, last):
            rank = jnp.broadcast_to(rank_row[s][0:1], (BLOCK, rows))
            hit = jnp.where(token_row + float(b * BLOCK) == rank, 1.0, 0.0)
            pick[b, :, (s - first) * rows : (s - first + 1) * rows] = hit.astype(BF16)

    def place_step(s, carry):
        rank = jnp.broadcast_to(rank_row[s][0:1], (rows, rows)).T
        rank = jnp.concatenate([rank] * (routed // rows), axis=1)
        place[s] = jnp.where(token_lane == rank, 1.0, 0.0).astype(BF16)
        return carry

    lax.fori_loop(0, n_ctx, place_step, 0)

    def packed(all_ref, b):
        first, last = slots_of(b)
        source = all_ref[first:last]
        width = (last - first) * rows
        return dot(pick[b, :, 0:width], source.reshape(width, source.shape[2])).astype(BF16)

    def span(b, e=1):
        return slice(b * BLOCK, (b + e) * BLOCK)

    local[2].wait()
    local[3].wait()
    arrived(v_all.at[few], CH_K)
    arrived(v_all.at[few], CH_Q)
    for b in range(blocks):
        kq_c[span(b)] = packed(kq_all, b)
    for b in range(blocks):
        kt_c[:, span(b)] = kq_c[span(b), 0:HEAD].astype(F32).T.astype(BF16)

    key_at = lax.broadcasted_iota(jnp.int32, (BLOCK, BLOCK), 0)
    query_at = lax.broadcasted_iota(jnp.int32, (BLOCK, BLOCK), 1)
    causal = key_at <= query_at
    for i in range(blocks):
        q_i = kq_c[span(i), HEAD : 2 * HEAD]
        parts = [dot_nt(kq_c[span(j), 0:HEAD], q_i) for j in range(i + 1)]
        parts[i] = jnp.where(causal, parts[i], NEG_FILL)
        top = functools.reduce(jnp.maximum, [jnp.max(s, axis=0, keepdims=True) for s in parts])
        parts = [jnp.exp2((s - top) * (scale * LOG2E)) for s in parts]
        total = functools.reduce(jnp.add, [jnp.sum(e, axis=0, keepdims=True) for e in parts])
        inverse = 1.0 / total
        for j in range(i + 1):
            p_buf[span(j), span(i)] = (parts[j] * inverse).astype(BF16)

    local[4].wait()
    arrived(v_all.at[few], CH_V)
    for b in range(blocks):
        v_c[span(b)] = packed(v_all, b)

    arrived(d_all.at[few], CH_D)
    for b in range(blocks):
        d_c[span(b)] = packed(d_all, b)

    for j in range(blocks):
        rest = slice(j * BLOCK, routed)
        gv_c[span(j)] = dot(p_buf[span(j), rest], d_c[rest]).astype(BF16)

    def unpacked(m, source, low, high):
        begin = max(0, (m + 1) * BLOCK - BLOCK - routed)
        end = min(routed, (m + 1) * BLOCK)
        hits = place[m * per_block : (m + 1) * per_block].reshape(BLOCK, routed)
        return dot(hits[:, begin:end], source[begin:end, low:high])

    pairs = n_ctx // per_block
    for m in range(pairs):
        both = unpacked(m, gv_c, 0, HEAD).astype(BF16).reshape(per_block, rows, HEAD)
        gv_send[m * per_block : (m + 1) * per_block] = both

    delta_slots = [jnp.zeros((8, rows), F32) for _ in range(n_ctx)]
    for i in range(blocks):
        d_i = d_c[span(i)]
        terms, weights = [], []
        for j in range(i + 1):
            p_ji = p_buf[span(j), span(i)].astype(F32)
            weights.append(p_ji)
            terms.append(p_ji * dot_nt(v_c[span(j)], d_i))
        delta = functools.reduce(jnp.add, [jnp.sum(t, axis=0, keepdims=True) for t in terms])
        for j in range(i + 1):
            ds_buf[span(j), span(i)] = (terms[j] - weights[j] * delta).astype(BF16)
        first, last = slots_of(i)
        width = (last - first) * rows
        moved = dot(three_rows(jnp.broadcast_to(delta, (8, BLOCK))), pick[i, :, 0:width])
        for s in range(first, last):
            delta_slots[s] = delta_slots[s] + moved[:, (s - first) * rows : (s - first + 1) * rows]
    for s in range(n_ctx):
        delta_send[s] = jnp.sum(delta_slots[s], axis=0, keepdims=True)
    delta_all[me] = delta_send[me]

    to_peers(lambda p: gv_send.at[p], cols(gv_ref, me), CH_GV, "ctx", n_ctx, me)
    to_peers(lambda p: delta_send.at[p], delta_all.at[me], CH_DELTA, "ctx", n_ctx, me)

    for j in range(blocks):
        rest = slice(j * BLOCK, routed)
        gkq_c[span(j), 0:HEAD] = (dot(ds_buf[span(j), rest], kq_c[rest, HEAD : 2 * HEAD]) * scale).astype(BF16)
    for i in range(blocks):
        upto = slice(0, (i + 1) * BLOCK)
        gkq_c[span(i), HEAD : 2 * HEAD] = (dot(kt_c[:, upto], ds_buf[upto, span(i)]) * scale).T.astype(BF16)
    for m in range(pairs):
        both = unpacked(m, gkq_c, 0, 2 * HEAD).astype(BF16)
        gk_send[m * per_block : (m + 1) * per_block] = both[:, 0:HEAD].reshape(per_block, rows, HEAD)
        gq_send[m * per_block : (m + 1) * per_block] = both[:, HEAD : 2 * HEAD].reshape(per_block, rows, HEAD)

    arrived(delta_all.at[few], CH_DELTA)
    row_sum = delta_all[0]
    for h in range(1, n_ctx):
        row_sum += delta_all[h]
    row_sum = jnp.broadcast_to(row_sum, (8, rows))
    split = three_rows(row_sum * (1.0 - gate_row))
    for p in range(n_dp):
        term_send[p] = jnp.sum(dot(split, x_v[:, p * chunk : (p + 1) * chunk]), axis=0, keepdims=True)
    term_y[me_y] = term_send[own_y]
    for o in range(1, n_y):
        group = pl.ds(lax.rem(me_y + o, n_y) * n_z, n_z)
        remote(term_send.at[group], term_y.at[me_y], CH_TERM_Y, "dp", y_peer(o)).start()
    to_peers(lambda p: gk_send.at[p], cols(gk_ref, me), CH_GK, "ctx", n_ctx, me)
    own = [
        pltpu.make_async_copy(gq_send.at[me], cols(gq_ref, me), local_sem.at[5]),
        pltpu.make_async_copy(gk_send.at[me], cols(gk_ref, me), local_sem.at[6]),
        pltpu.make_async_copy(gv_send.at[me], cols(gv_ref, me), local_sem.at[7]),
    ]
    for copy in own:
        copy.start()
    if n_y > 1:
        arrived(term_y.at[pl.ds(0, n_y - 1)], CH_TERM_Y)
    half = term_y[0]
    for p in range(1, n_y):
        half += term_y[p]
    term_half[...] = half
    term_z[me_z] = term_half[me_z]
    for o in range(1, n_z):
        remote(term_half.at[lax.rem(me_z + o, n_z)], term_z.at[me_z], CH_TERM_Z, "dp", z_peer(o)).start()
    if n_z > 1:
        arrived(term_z.at[pl.ds(0, n_z - 1)], CH_TERM_Z)
    term_sum = term_z[0]
    for p in range(1, n_z):
        term_sum += term_z[p]
    sum_send[...] = term_sum
    sum_all[me] = term_sum
    to_peers(lambda p: sum_send, sum_all.at[me], CH_SUM, "ctx", n_ctx, me)
    to_peers(lambda p: gq_send.at[p], cols(gq_ref, me), CH_GQ, "ctx", n_ctx, me)
    arrived(sum_all.at[few], CH_SUM)
    everything = sum_all[0]
    for c in range(1, n_ctx):
        everything += sum_all[c]
    rg_ref[...] = everything * (1.0 / total_routed)

    most = pl.ds(0, (n_ctx - 1) * HEAD)
    arrived(gv_ref.at[:, most], CH_GV)
    arrived(gk_ref.at[:, most], CH_GK)
    arrived(gq_ref.at[:, most], CH_GQ)
    for copy in own:
        copy.wait()
    for ref, channel in (
        (v_all, CH_K),
        (v_all, CH_Q),
        (v_all, CH_V),
        (d_all, CH_D),
        (live_all, CH_LIVE),
        (delta_all, CH_DELTA),
        (sum_all, CH_SUM),
        (gq_send, CH_GQ),
        (gk_send, CH_GK),
        (gv_send, CH_GV),
    ):
        sent(ref.at[few], channel)
    if n_z > 1:
        sent(w_all.at[pl.ds(0, n_z - 1)], CH_W_Z)
        sent(term_z.at[pl.ds(0, n_z - 1)], CH_TERM_Z)
    if n_y > 1:
        sent(w_all.at[pl.ds(0, (n_y - 1) * n_z)], CH_W_Y)
        sent(term_y.at[pl.ds(0, n_y - 1)], CH_TERM_Y)


def widen(gq_ref, gk_ref, gv_ref, rg_ref, q_out, k_out, v_out, r_out):
    q_out[...] = gq_ref[...].astype(F32)
    k_out[...] = gk_ref[...].astype(F32)
    v_out[...] = gv_ref[...].astype(F32)
    r_out[...] = rg_ref[0]


def body(route_pos, x_routed, w_router, queries, keys, values, d_gated):
    n_ctx = lax.axis_size("ctx")
    n_dp = lax.axis_size("dp")
    n_z = 4 if n_dp >= 16 else min(2, n_dp)
    n_y = n_dp // n_z
    rows, width = queries.shape[1:]
    routed = n_ctx * rows // 2
    blocks = routed // BLOCK
    chunk = w_router.shape[0]
    vmem = pl.BlockSpec(memory_space=pltpu.VMEM)
    hbm = pl.BlockSpec(memory_space=pltpu.HBM)
    heads = pltpu.VMEM((n_ctx, rows, HEAD), BF16)
    small = pltpu.VMEM((n_ctx, 1, rows), F32)
    compact = pltpu.VMEM((routed, HEAD), BF16)
    square = pltpu.VMEM((routed, routed), BF16)
    out = jax.ShapeDtypeStruct((rows, width), BF16)
    gq, gk, gv, rg = pl.pallas_call(
        functools.partial(kernel, n_ctx, n_y, n_z),
        out_shape=(out, out, out, jax.ShapeDtypeStruct((1, chunk), F32)),
        in_specs=[vmem, vmem] + [hbm] * 5,
        out_specs=(hbm, hbm, hbm, vmem),
        scratch_shapes=[
            pltpu.VMEM(x_routed.shape[1:], BF16),
            pltpu.VMEM((rows, width), F32),
            heads,
            pltpu.VMEM((n_ctx, rows, 2 * HEAD), BF16),
            heads,
            heads,
            small,
            pltpu.VMEM((1, rows), F32),
            pltpu.VMEM((n_dp, 1, chunk), BF16),
            pltpu.VMEM((n_ctx, 8, rows), F32),
            pltpu.VMEM((blocks, BLOCK, routed + BLOCK), BF16),
            pltpu.VMEM((n_ctx, rows, routed), BF16),
            pltpu.VMEM((routed, 2 * HEAD), BF16),
            pltpu.VMEM((HEAD, routed), BF16),
            compact,
            compact,
            square,
            square,
            pltpu.VMEM((routed, 2 * HEAD), BF16),
            compact,
            small,
            small,
            heads,
            heads,
            heads,
            pltpu.VMEM((n_dp, 1, chunk), F32),
            pltpu.VMEM((n_y, n_z, 1, chunk), F32),
            pltpu.VMEM((n_z, 1, chunk), F32),
            pltpu.VMEM((n_z, 1, chunk), F32),
            pltpu.VMEM((1, chunk), F32),
            pltpu.VMEM((n_ctx, 1, chunk), F32),
            pltpu.SemaphoreType.DMA((8,)),
            pltpu.SemaphoreType.DMA((CHANNELS,)),
            pltpu.SemaphoreType.DMA((CHANNELS,)),
        ],
        compiler_params=pltpu.CompilerParams(collective_id=0, has_side_effects=True, vmem_limit_bytes=60 * 1024 * 1024),
        name="routed_backward",
    )(route_pos, w_router, x_routed[0], queries[0], keys[0], values[0], d_gated[0])
    steps = 4
    tile = pl.BlockSpec((rows // steps, width), lambda i: (i, 0))
    wide = jax.ShapeDtypeStruct((rows, width), F32)
    gq, gk, gv, rg = pl.pallas_call(
        widen,
        grid=(steps,),
        out_shape=(wide, wide, wide, jax.ShapeDtypeStruct((chunk,), F32)),
        in_specs=[tile, tile, tile, pl.BlockSpec((1, chunk), lambda i: (0, 0))],
        out_specs=(tile, tile, tile, pl.BlockSpec((chunk,), lambda i: (0,))),
        name="widen",
    )(gq, gk, gv, rg)
    return (gq[None], gk[None], gv[None], rg)


def solution(mesh):
    placed = (
        P("dp", "ctx"),
        P("dp", "ctx", None),
        P("dp"),
        P("dp", "ctx", None),
        P("dp", "ctx", None),
        P("dp", "ctx", None),
        P("dp", "ctx", None),
    )
    return jax.shard_map(
        body,
        mesh=mesh,
        in_specs=placed,
        out_specs=(P("dp", "ctx", None), P("dp", "ctx", None), P("dp", "ctx", None), P("dp")),
        check_vma=False,
    )
```

```python
import functools

import jax
import jax.numpy as jnp
from jax import lax
from jax.experimental import pallas as pl
from jax.experimental.pallas import tpu as pltpu
from jax.sharding import PartitionSpec as P

HEAD = 128
NEG_FILL = -1e30
LOG2E = 1.4426950408889634
MESH = pl.DeviceIdType.MESH
F32 = jnp.float32
BF16 = jnp.bfloat16
BLOCK = 256
NT = (((1,), (1,)), ((), ()))
GROUPS = (
    ((1, 0, 0), (3, 0, 0), (0, 1, 0), (2, 1, 1), (2, 0, 0)),
    ((1, 0, 1), (3, 0, 1), (0, 1, 1), (2, 0, 1), (1, 1, 0)),
    ((3, 1, 0), (1, 1, 1), (3, 1, 1), (2, 1, 0), (0, 0, 1)),
)
EVERY = GROUPS[0] + GROUPS[1] + GROUPS[2]
CH_K, CH_Q, CH_V, CH_D, CH_LIVE, CH_W_Z, CH_W_Y, CH_DELTA, CH_TERM_Y, CH_TERM_Z, CH_SUM, CH_GQ, CH_GK, CH_GV = range(14)
CHANNELS = 14


def dot(a, b):
    return jnp.dot(a, b, preferred_element_type=F32)


def dot_nt(a, b):
    return lax.dot_general(a, b, NT, preferred_element_type=F32)


def three_rows(row):
    high = row.astype(BF16).astype(F32)
    middle = (row - high).astype(BF16).astype(F32)
    low = row - high - middle
    which = lax.broadcasted_iota(jnp.int32, row.shape, 0)
    split = jnp.where(which == 0, high, jnp.where(which == 1, middle, low))
    return jnp.where(which < 3, split, 0.0).astype(BF16)


def kernel(
    n_ctx,
    n_y,
    n_z,
    pos_ref,
    w_ref,
    x_hbm,
    q_hbm,
    k_hbm,
    v_hbm,
    d_hbm,
    gq_ref,
    gk_ref,
    gv_ref,
    rg_ref,
    x_v,
    d_v,
    d_send,
    kq_all,
    v_all,
    d_all,
    live_all,
    live_own,
    w_all,
    rank_row,
    pick,
    place,
    kq_c,
    kt_c,
    v_c,
    d_c,
    p_buf,
    ds_buf,
    gkq_c,
    gv_c,
    delta_send,
    delta_all,
    gq_send,
    gk_send,
    gv_send,
    term_send,
    term_y,
    term_half,
    term_z,
    sum_send,
    sum_all,
    local_sem,
    send_sem,
    recv_sem,
):
    me = lax.axis_index("ctx")
    me_dp = lax.axis_index("dp")
    n_dp = n_y * n_z
    me_y, me_z = me_dp // n_z, lax.rem(me_dp, n_z)
    rows = q_hbm.shape[0]
    slots = n_ctx * rows
    routed = slots // 2
    blocks = routed // BLOCK
    per_block = BLOCK // rows
    scale = HEAD ** (-0.5)
    chunk = w_all.shape[2]
    total_routed = float(n_dp * routed)

    def z_peer(o):
        return me_y * n_z + lax.rem(me_z + o, n_z)

    def y_peer(o):
        return lax.rem(me_y + o, n_y) * n_z + me_z

    barrier = pltpu.get_barrier_semaphore()
    for o in range(1, n_z):
        pl.semaphore_signal(barrier, inc=1, device_id={"dp": z_peer(o)}, device_id_type=MESH)
    for o in range(1, n_y):
        pl.semaphore_signal(barrier, inc=1, device_id={"dp": y_peer(o)}, device_id_type=MESH)
    for o in range(1, n_ctx):
        pl.semaphore_signal(barrier, inc=1, device_id={"ctx": lax.rem(me + o, n_ctx)}, device_id_type=MESH)

    def cols(ref, at):
        return ref.at[:, pl.ds(pl.multiple_of(at * HEAD, HEAD), HEAD)]

    local = [
        pltpu.make_async_copy(d_hbm, d_v, local_sem.at[0]),
        pltpu.make_async_copy(x_hbm, x_v, local_sem.at[1]),
        pltpu.make_async_copy(cols(k_hbm, me), kq_all.at[me, :, pl.ds(0, HEAD)], local_sem.at[2]),
        pltpu.make_async_copy(cols(q_hbm, me), kq_all.at[me, :, pl.ds(HEAD, HEAD)], local_sem.at[3]),
        pltpu.make_async_copy(cols(v_hbm, me), v_all.at[me], local_sem.at[4]),
    ]
    for copy in local:
        copy.start()

    def remote(src, dst, channel, axis, peer):
        return pltpu.make_async_remote_copy(
            src_ref=src,
            dst_ref=dst,
            send_sem=send_sem.at[channel],
            recv_sem=recv_sem.at[channel],
            device_id={axis: peer},
            device_id_type=MESH,
        )

    def to_peers(source_of, dst, channel, group=EVERY):
        for dx, dz, dc in group:
            peer = 4 * lax.rem(me // 4 + dx, n_ctx // 4) + 2 * lax.rem(me // 2 + dz, 2) + lax.rem(me + dc, 2)
            remote(source_of(peer), dst, channel, "ctx", peer).start()

    def arrived(ref, channel):
        remote(ref, ref, channel, "ctx", lax.rem(me + 1, n_ctx)).wait_recv()

    def sent(ref, channel):
        remote(ref, ref, channel, "ctx", lax.rem(me + 1, n_ctx)).wait_send()

    few = pl.ds(0, n_ctx - 1)

    live_row = jnp.where(jnp.broadcast_to(pos_ref[...], (8, rows)) >= 0, 1.0, 0.0).astype(F32)
    live_own[...] = live_row[0:1]
    live_all[me] = live_row[0:1]
    w_all[me_dp] = w_ref[...].reshape(1, chunk)

    pl.semaphore_wait(barrier, n_ctx + n_y + n_z - 3)

    for o in range(1, n_z):
        remote(w_all.at[me_dp], w_all.at[me_dp], CH_W_Z, "dp", z_peer(o)).start()
    to_peers(lambda p: live_own, live_all.at[me], CH_LIVE)
    to_peers(lambda p: cols(k_hbm, p), kq_all.at[me, :, pl.ds(0, HEAD)], CH_K)
    to_peers(lambda p: cols(q_hbm, p), kq_all.at[me, :, pl.ds(HEAD, HEAD)], CH_Q)
    to_peers(lambda p: cols(v_hbm, p), v_all.at[me], CH_V)

    local[1].wait()
    if n_z > 1:
        arrived(w_all.at[pl.ds(0, n_z - 1)], CH_W_Z)
    own_y = pl.ds(me_y * n_z, n_z)
    for o in range(1, n_y):
        remote(w_all.at[own_y], w_all.at[own_y], CH_W_Y, "dp", y_peer(o)).start()
    if n_y > 1:
        arrived(w_all.at[pl.ds(0, (n_y - 1) * n_z)], CH_W_Y)
    logit = jnp.zeros((rows, rows), F32)
    for p in range(n_dp):
        w_p = jnp.broadcast_to(w_all[p].astype(F32), (rows, chunk)).astype(BF16)
        logit += dot_nt(x_v[:, p * chunk : (p + 1) * chunk], w_p)
    gate = jax.nn.sigmoid(logit)
    gate_row = gate.T[0:8]
    factor = gate * jnp.broadcast_to(live_row[0:1], (rows, rows)).T
    local[0].wait()
    for h in range(n_ctx):
        d_send[h] = (d_v[:, h * HEAD : (h + 1) * HEAD] * factor).astype(BF16)
    d_all[me] = d_send[me]

    arrived(live_all.at[few], CH_LIVE)
    lane = lax.broadcasted_iota(jnp.int32, (8, rows), 1).astype(F32)
    before = jnp.zeros((8, rows), F32)
    for s in range(n_ctx):
        live_s = jnp.broadcast_to(live_all[s], (8, rows))
        rank_row[s] = jnp.where(live_s > 0.0, before + lane, -1.0)
        before = before + jnp.sum(live_s, axis=1, keepdims=True)

    to_peers(lambda p: d_send.at[p], d_all.at[me], CH_D)

    token_row = lax.broadcasted_iota(jnp.int32, (BLOCK, rows), 0).astype(F32)
    token_lane = lax.broadcasted_iota(jnp.int32, (rows, routed), 1).astype(F32)

    def slots_of(b):
        first = b * per_block
        return first, min(n_ctx, first + (routed + BLOCK) // rows)

    for b in range(blocks):
        first, last = slots_of(b)
        for s in range(first, last):
            rank = jnp.broadcast_to(rank_row[s][0:1], (BLOCK, rows))
            hit = jnp.where(token_row + float(b * BLOCK) == rank, 1.0, 0.0)
            pick[b, :, (s - first) * rows : (s - first + 1) * rows] = hit.astype(BF16)

    def place_step(s, carry):
        rank = jnp.broadcast_to(rank_row[s][0:1], (rows, rows)).T
        rank = jnp.concatenate([rank] * (routed // rows), axis=1)
        place[s] = jnp.where(token_lane == rank, 1.0, 0.0).astype(BF16)
        return carry

    lax.fori_loop(0, n_ctx, place_step, 0)

    def packed(all_ref, b):
        first, last = slots_of(b)
        source = all_ref[first:last]
        width = (last - first) * rows
        return dot(pick[b, :, 0:width], source.reshape(width, source.shape[2])).astype(BF16)

    def span(b, e=1):
        return slice(b * BLOCK, (b + e) * BLOCK)

    local[2].wait()
    local[3].wait()
    arrived(v_all.at[few], CH_K)
    arrived(v_all.at[few], CH_Q)
    for b in range(blocks):
        kq_c[span(b)] = packed(kq_all, b)
    for b in range(blocks):
        kt_c[:, span(b)] = kq_c[span(b), 0:HEAD].astype(F32).T.astype(BF16)

    key_at = lax.broadcasted_iota(jnp.int32, (BLOCK, BLOCK), 0)
    query_at = lax.broadcasted_iota(jnp.int32, (BLOCK, BLOCK), 1)
    causal = key_at <= query_at
    for i in range(blocks):
        q_i = kq_c[span(i), HEAD : 2 * HEAD]
        parts = [dot_nt(kq_c[span(j), 0:HEAD], q_i) for j in range(i + 1)]
        parts[i] = jnp.where(causal, parts[i], NEG_FILL)
        top = functools.reduce(jnp.maximum, [jnp.max(s, axis=0, keepdims=True) for s in parts])
        parts = [jnp.exp2((s - top) * (scale * LOG2E)) for s in parts]
        total = functools.reduce(jnp.add, [jnp.sum(e, axis=0, keepdims=True) for e in parts])
        inverse = 1.0 / total
        for j in range(i + 1):
            p_buf[span(j), span(i)] = (parts[j] * inverse).astype(BF16)

    local[4].wait()
    arrived(v_all.at[few], CH_V)
    for b in range(blocks):
        v_c[span(b)] = packed(v_all, b)

    arrived(d_all.at[few], CH_D)
    for b in range(blocks):
        d_c[span(b)] = packed(d_all, b)

    for j in range(blocks):
        rest = slice(j * BLOCK, routed)
        gv_c[span(j)] = dot(p_buf[span(j), rest], d_c[rest]).astype(BF16)

    def unpacked(m, source, low, high):
        begin = max(0, (m + 1) * BLOCK - BLOCK - routed)
        end = min(routed, (m + 1) * BLOCK)
        hits = place[m * per_block : (m + 1) * per_block].reshape(BLOCK, routed)
        return dot(hits[:, begin:end], source[begin:end, low:high])

    pairs = n_ctx // per_block
    for m in range(pairs):
        both = unpacked(m, gv_c, 0, HEAD).astype(BF16).reshape(per_block, rows, HEAD)
        gv_send[m * per_block : (m + 1) * per_block] = both

    to_peers(lambda p: gv_send.at[p], cols(gv_ref, me), CH_GV, GROUPS[0])

    delta_slots = [jnp.zeros((8, rows), F32) for _ in range(n_ctx)]
    for i in range(blocks):
        d_i = d_c[span(i)]
        terms, weights = [], []
        for j in range(i + 1):
            p_ji = p_buf[span(j), span(i)].astype(F32)
            weights.append(p_ji)
            terms.append(p_ji * dot_nt(v_c[span(j)], d_i))
        delta = functools.reduce(jnp.add, [jnp.sum(t, axis=0, keepdims=True) for t in terms])
        for j in range(i + 1):
            ds_buf[span(j), span(i)] = (terms[j] - weights[j] * delta).astype(BF16)
        first, last = slots_of(i)
        width = (last - first) * rows
        moved = dot(three_rows(jnp.broadcast_to(delta, (8, BLOCK))), pick[i, :, 0:width])
        for s in range(first, last):
            delta_slots[s] = delta_slots[s] + moved[:, (s - first) * rows : (s - first + 1) * rows]
    for s in range(n_ctx):
        delta_send[s] = jnp.sum(delta_slots[s], axis=0, keepdims=True)
    delta_all[me] = delta_send[me]

    to_peers(lambda p: delta_send.at[p], delta_all.at[me], CH_DELTA)
    to_peers(lambda p: gv_send.at[p], cols(gv_ref, me), CH_GV, GROUPS[1] + GROUPS[2])

    for j in range(blocks):
        rest = slice(j * BLOCK, routed)
        gkq_c[span(j), 0:HEAD] = (dot(ds_buf[span(j), rest], kq_c[rest, HEAD : 2 * HEAD]) * scale).astype(BF16)
    for i in range(blocks):
        upto = slice(0, (i + 1) * BLOCK)
        gkq_c[span(i), HEAD : 2 * HEAD] = (dot(kt_c[:, upto], ds_buf[upto, span(i)]) * scale).T.astype(BF16)
    for m in range(pairs):
        both = unpacked(m, gkq_c, 0, 2 * HEAD).astype(BF16)
        gk_send[m * per_block : (m + 1) * per_block] = both[:, 0:HEAD].reshape(per_block, rows, HEAD)
        gq_send[m * per_block : (m + 1) * per_block] = both[:, HEAD : 2 * HEAD].reshape(per_block, rows, HEAD)

    arrived(delta_all.at[few], CH_DELTA)
    row_sum = delta_all[0]
    for h in range(1, n_ctx):
        row_sum += delta_all[h]
    row_sum = jnp.broadcast_to(row_sum, (8, rows))
    split = three_rows(row_sum * (1.0 - gate_row))
    for p in range(n_dp):
        term_send[p] = jnp.sum(dot(split, x_v[:, p * chunk : (p + 1) * chunk]), axis=0, keepdims=True)
    term_y[me_y] = term_send[own_y]
    for o in range(1, n_y):
        group = pl.ds(lax.rem(me_y + o, n_y) * n_z, n_z)
        remote(term_send.at[group], term_y.at[me_y], CH_TERM_Y, "dp", y_peer(o)).start()
    to_peers(lambda p: gk_send.at[p], cols(gk_ref, me), CH_GK, GROUPS[0] + GROUPS[1])
    if n_y > 1:
        arrived(term_y.at[pl.ds(0, n_y - 1)], CH_TERM_Y)
    half = term_y[0]
    for p in range(1, n_y):
        half += term_y[p]
    term_half[...] = half
    term_z[me_z] = term_half[me_z]
    for o in range(1, n_z):
        remote(term_half.at[lax.rem(me_z + o, n_z)], term_z.at[me_z], CH_TERM_Z, "dp", z_peer(o)).start()
    to_peers(lambda p: gk_send.at[p], cols(gk_ref, me), CH_GK, GROUPS[2])
    to_peers(lambda p: gq_send.at[p], cols(gq_ref, me), CH_GQ, GROUPS[0])
    if n_z > 1:
        arrived(term_z.at[pl.ds(0, n_z - 1)], CH_TERM_Z)
    term_sum = term_z[0]
    for p in range(1, n_z):
        term_sum += term_z[p]
    sum_send[...] = term_sum
    sum_all[me] = term_sum
    to_peers(lambda p: sum_send, sum_all.at[me], CH_SUM)
    to_peers(lambda p: gq_send.at[p], cols(gq_ref, me), CH_GQ, GROUPS[1] + GROUPS[2])
    own = [
        pltpu.make_async_copy(gq_send.at[me], cols(gq_ref, me), local_sem.at[5]),
        pltpu.make_async_copy(gk_send.at[me], cols(gk_ref, me), local_sem.at[6]),
        pltpu.make_async_copy(gv_send.at[me], cols(gv_ref, me), local_sem.at[7]),
    ]
    for copy in own:
        copy.start()
    arrived(sum_all.at[few], CH_SUM)
    everything = sum_all[0]
    for c in range(1, n_ctx):
        everything += sum_all[c]
    rg_ref[...] = everything * (1.0 / total_routed)

    most = pl.ds(0, (n_ctx - 1) * HEAD)
    arrived(gv_ref.at[:, most], CH_GV)
    arrived(gk_ref.at[:, most], CH_GK)
    arrived(gq_ref.at[:, most], CH_GQ)
    for copy in own:
        copy.wait()
    for ref, channel in (
        (v_all, CH_K),
        (v_all, CH_Q),
        (v_all, CH_V),
        (d_all, CH_D),
        (live_all, CH_LIVE),
        (delta_all, CH_DELTA),
        (sum_all, CH_SUM),
        (gq_send, CH_GQ),
        (gk_send, CH_GK),
        (gv_send, CH_GV),
    ):
        sent(ref.at[few], channel)
    if n_z > 1:
        sent(w_all.at[pl.ds(0, n_z - 1)], CH_W_Z)
        sent(term_z.at[pl.ds(0, n_z - 1)], CH_TERM_Z)
    if n_y > 1:
        sent(w_all.at[pl.ds(0, (n_y - 1) * n_z)], CH_W_Y)
        sent(term_y.at[pl.ds(0, n_y - 1)], CH_TERM_Y)


def widen(gq_ref, gk_ref, gv_ref, rg_ref, q_out, k_out, v_out, r_out):
    q_out[...] = gq_ref[...].astype(F32)
    k_out[...] = gk_ref[...].astype(F32)
    v_out[...] = gv_ref[...].astype(F32)
    r_out[...] = rg_ref[0]


def body(route_pos, x_routed, w_router, queries, keys, values, d_gated):
    n_ctx = lax.axis_size("ctx")
    n_dp = lax.axis_size("dp")
    n_z = 4 if n_dp >= 16 else min(2, n_dp)
    n_y = n_dp // n_z
    rows, width = queries.shape[1:]
    routed = n_ctx * rows // 2
    blocks = routed // BLOCK
    chunk = w_router.shape[0]
    vmem = pl.BlockSpec(memory_space=pltpu.VMEM)
    hbm = pl.BlockSpec(memory_space=pltpu.HBM)
    heads = pltpu.VMEM((n_ctx, rows, HEAD), BF16)
    small = pltpu.VMEM((n_ctx, 1, rows), F32)
    compact = pltpu.VMEM((routed, HEAD), BF16)
    square = pltpu.VMEM((routed, routed), BF16)
    out = jax.ShapeDtypeStruct((rows, width), BF16)
    gq, gk, gv, rg = pl.pallas_call(
        functools.partial(kernel, n_ctx, n_y, n_z),
        out_shape=(out, out, out, jax.ShapeDtypeStruct((1, chunk), F32)),
        in_specs=[vmem, vmem] + [hbm] * 5,
        out_specs=(hbm, hbm, hbm, vmem),
        scratch_shapes=[
            pltpu.VMEM(x_routed.shape[1:], BF16),
            pltpu.VMEM((rows, width), F32),
            heads,
            pltpu.VMEM((n_ctx, rows, 2 * HEAD), BF16),
            heads,
            heads,
            small,
            pltpu.VMEM((1, rows), F32),
            pltpu.VMEM((n_dp, 1, chunk), BF16),
            pltpu.VMEM((n_ctx, 8, rows), F32),
            pltpu.VMEM((blocks, BLOCK, routed + BLOCK), BF16),
            pltpu.VMEM((n_ctx, rows, routed), BF16),
            pltpu.VMEM((routed, 2 * HEAD), BF16),
            pltpu.VMEM((HEAD, routed), BF16),
            compact,
            compact,
            square,
            square,
            pltpu.VMEM((routed, 2 * HEAD), BF16),
            compact,
            small,
            small,
            heads,
            heads,
            heads,
            pltpu.VMEM((n_dp, 1, chunk), F32),
            pltpu.VMEM((n_y, n_z, 1, chunk), F32),
            pltpu.VMEM((n_z, 1, chunk), F32),
            pltpu.VMEM((n_z, 1, chunk), F32),
            pltpu.VMEM((1, chunk), F32),
            pltpu.VMEM((n_ctx, 1, chunk), F32),
            pltpu.SemaphoreType.DMA((8,)),
            pltpu.SemaphoreType.DMA((CHANNELS,)),
            pltpu.SemaphoreType.DMA((CHANNELS,)),
        ],
        compiler_params=pltpu.CompilerParams(collective_id=0, has_side_effects=True, vmem_limit_bytes=60 * 1024 * 1024),
        name="routed_backward",
    )(route_pos, w_router, x_routed[0], queries[0], keys[0], values[0], d_gated[0])
    steps = 4
    tile = pl.BlockSpec((rows // steps, width), lambda i: (i, 0))
    wide = jax.ShapeDtypeStruct((rows, width), F32)
    gq, gk, gv, rg = pl.pallas_call(
        widen,
        grid=(steps,),
        out_shape=(wide, wide, wide, jax.ShapeDtypeStruct((chunk,), F32)),
        in_specs=[tile, tile, tile, pl.BlockSpec((1, chunk), lambda i: (0, 0))],
        out_specs=(tile, tile, tile, pl.BlockSpec((chunk,), lambda i: (0,))),
        name="widen",
    )(gq, gk, gv, rg)
    return (gq[None], gk[None], gv[None], rg)


def solution(mesh):
    placed = (
        P("dp", "ctx"),
        P("dp", "ctx", None),
        P("dp"),
        P("dp", "ctx", None),
        P("dp", "ctx", None),
        P("dp", "ctx", None),
        P("dp", "ctx", None),
    )
    return jax.shard_map(
        body,
        mesh=mesh,
        in_specs=placed,
        out_specs=(P("dp", "ctx", None), P("dp", "ctx", None), P("dp", "ctx", None), P("dp")),
        check_vma=False,
    )
```

```python
import functools

import jax
import jax.numpy as jnp
from jax import lax
from jax.experimental import pallas as pl
from jax.experimental.pallas import tpu as pltpu
from jax.sharding import PartitionSpec as P

HEAD = 128
NEG_FILL = -1e30
LOG2E = 1.4426950408889634
MESH = pl.DeviceIdType.MESH
F32 = jnp.float32
BF16 = jnp.bfloat16
BLOCK = 256
NT = (((1,), (1,)), ((), ()))
GROUPS = (
    ((1, 0, 0), (3, 0, 0), (0, 1, 0), (2, 1, 1), (2, 0, 0)),
    ((1, 0, 1), (3, 0, 1), (0, 1, 1), (2, 0, 1), (1, 1, 0)),
    ((3, 1, 0), (1, 1, 1), (3, 1, 1), (2, 1, 0), (0, 0, 1)),
)
EVERY = GROUPS[0] + GROUPS[1] + GROUPS[2]
CH_K, CH_Q, CH_V, CH_D, CH_LIVE, CH_W_Z, CH_W_Y, CH_DELTA, CH_TERM_Y, CH_TERM_Z, CH_SUM, CH_GQ, CH_GK, CH_GV = range(14)
CHANNELS = 14


def dot(a, b):
    return jnp.dot(a, b, preferred_element_type=F32)


def dot_nt(a, b):
    return lax.dot_general(a, b, NT, preferred_element_type=F32)


def three_rows(row):
    high = row.astype(BF16).astype(F32)
    middle = (row - high).astype(BF16).astype(F32)
    low = row - high - middle
    which = lax.broadcasted_iota(jnp.int32, row.shape, 0)
    split = jnp.where(which == 0, high, jnp.where(which == 1, middle, low))
    return jnp.where(which < 3, split, 0.0).astype(BF16)


def kernel(
    n_ctx,
    n_y,
    n_z,
    pos_ref,
    w_ref,
    x_hbm,
    q_hbm,
    k_hbm,
    v_hbm,
    d_hbm,
    gq_ref,
    gk_ref,
    gv_ref,
    rg_ref,
    x_v,
    d_v,
    d_send,
    kq_all,
    v_all,
    d_all,
    live_all,
    live_own,
    w_all,
    rank_row,
    pick,
    place,
    kq_c,
    kt_c,
    v_c,
    d_c,
    p_buf,
    ds_buf,
    gkq_c,
    gv_c,
    delta_send,
    delta_all,
    gq_send,
    gk_send,
    gv_send,
    term_send,
    term_y,
    term_half,
    term_z,
    sum_send,
    sum_all,
    local_sem,
    send_sem,
    recv_sem,
):
    me = lax.axis_index("ctx")
    me_dp = lax.axis_index("dp")
    n_dp = n_y * n_z
    me_y, me_z = me_dp // n_z, lax.rem(me_dp, n_z)
    rows = q_hbm.shape[0]
    slots = n_ctx * rows
    routed = slots // 2
    blocks = routed // BLOCK
    per_block = BLOCK // rows
    scale = HEAD ** (-0.5)
    chunk = w_all.shape[2]
    total_routed = float(n_dp * routed)

    def z_peer(o):
        return me_y * n_z + lax.rem(me_z + o, n_z)

    def y_peer(o):
        return lax.rem(me_y + o, n_y) * n_z + me_z

    barrier = pltpu.get_barrier_semaphore()
    for o in range(1, n_z):
        pl.semaphore_signal(barrier, inc=1, device_id={"dp": z_peer(o)}, device_id_type=MESH)
    for o in range(1, n_y):
        pl.semaphore_signal(barrier, inc=1, device_id={"dp": y_peer(o)}, device_id_type=MESH)
    for o in range(1, n_ctx):
        pl.semaphore_signal(barrier, inc=1, device_id={"ctx": lax.rem(me + o, n_ctx)}, device_id_type=MESH)

    def cols(ref, at):
        return ref.at[:, pl.ds(pl.multiple_of(at * HEAD, HEAD), HEAD)]

    local = [
        pltpu.make_async_copy(d_hbm, d_v, local_sem.at[0]),
        pltpu.make_async_copy(x_hbm, x_v, local_sem.at[1]),
        pltpu.make_async_copy(cols(k_hbm, me), kq_all.at[me, :, pl.ds(0, HEAD)], local_sem.at[2]),
        pltpu.make_async_copy(cols(q_hbm, me), kq_all.at[me, :, pl.ds(HEAD, HEAD)], local_sem.at[3]),
        pltpu.make_async_copy(cols(v_hbm, me), v_all.at[me], local_sem.at[4]),
    ]
    for copy in local:
        copy.start()

    def remote(src, dst, channel, axis, peer):
        return pltpu.make_async_remote_copy(
            src_ref=src,
            dst_ref=dst,
            send_sem=send_sem.at[channel],
            recv_sem=recv_sem.at[channel],
            device_id={axis: peer},
            device_id_type=MESH,
        )

    def to_peers(source_of, dst, channel, group=EVERY):
        for dx, dz, dc in group:
            peer = 4 * lax.rem(me // 4 + dx, n_ctx // 4) + 2 * lax.rem(me // 2 + dz, 2) + lax.rem(me + dc, 2)
            remote(source_of(peer), dst, channel, "ctx", peer).start()

    def arrived(ref, channel):
        remote(ref, ref, channel, "ctx", lax.rem(me + 1, n_ctx)).wait_recv()

    def sent(ref, channel):
        remote(ref, ref, channel, "ctx", lax.rem(me + 1, n_ctx)).wait_send()

    few = pl.ds(0, n_ctx - 1)

    live_row = jnp.where(jnp.broadcast_to(pos_ref[...], (8, rows)) >= 0, 1.0, 0.0).astype(F32)
    live_own[...] = live_row[0:1]
    live_all[me] = live_row[0:1]
    w_all[me_dp] = w_ref[...].reshape(1, chunk)

    pl.semaphore_wait(barrier, n_ctx + n_y + n_z - 3)

    for o in range(1, n_z):
        remote(w_all.at[me_dp], w_all.at[me_dp], CH_W_Z, "dp", z_peer(o)).start()
    to_peers(lambda p: live_own, live_all.at[me], CH_LIVE)
    to_peers(lambda p: cols(k_hbm, p), kq_all.at[me, :, pl.ds(0, HEAD)], CH_K)
    to_peers(lambda p: cols(q_hbm, p), kq_all.at[me, :, pl.ds(HEAD, HEAD)], CH_Q)
    to_peers(lambda p: cols(v_hbm, p), v_all.at[me], CH_V, GROUPS[0])

    local[1].wait()
    if n_z > 1:
        arrived(w_all.at[pl.ds(0, n_z - 1)], CH_W_Z)
    own_y = pl.ds(me_y * n_z, n_z)
    for o in range(1, n_y):
        remote(w_all.at[own_y], w_all.at[own_y], CH_W_Y, "dp", y_peer(o)).start()
    if n_y > 1:
        arrived(w_all.at[pl.ds(0, (n_y - 1) * n_z)], CH_W_Y)
    logit = jnp.zeros((rows, rows), F32)
    for p in range(n_dp):
        w_p = jnp.broadcast_to(w_all[p].astype(F32), (rows, chunk)).astype(BF16)
        logit += dot_nt(x_v[:, p * chunk : (p + 1) * chunk], w_p)
    gate = jax.nn.sigmoid(logit)
    gate_row = gate.T[0:8]
    factor = gate * jnp.broadcast_to(live_row[0:1], (rows, rows)).T
    local[0].wait()
    for h in range(n_ctx):
        d_send[h] = (d_v[:, h * HEAD : (h + 1) * HEAD] * factor).astype(BF16)
    d_all[me] = d_send[me]

    arrived(live_all.at[few], CH_LIVE)
    lane = lax.broadcasted_iota(jnp.int32, (8, rows), 1).astype(F32)
    before = jnp.zeros((8, rows), F32)
    for s in range(n_ctx):
        live_s = jnp.broadcast_to(live_all[s], (8, rows))
        rank_row[s] = jnp.where(live_s > 0.0, before + lane, -1.0)
        before = before + jnp.sum(live_s, axis=1, keepdims=True)

    to_peers(lambda p: d_send.at[p], d_all.at[me], CH_D)
    to_peers(lambda p: cols(v_hbm, p), v_all.at[me], CH_V, GROUPS[1] + GROUPS[2])

    token_row = lax.broadcasted_iota(jnp.int32, (BLOCK, rows), 0).astype(F32)
    token_lane = lax.broadcasted_iota(jnp.int32, (rows, routed), 1).astype(F32)

    def slots_of(b):
        first = b * per_block
        return first, min(n_ctx, first + (routed + BLOCK) // rows)

    for b in range(blocks):
        first, last = slots_of(b)
        for s in range(first, last):
            rank = jnp.broadcast_to(rank_row[s][0:1], (BLOCK, rows))
            hit = jnp.where(token_row + float(b * BLOCK) == rank, 1.0, 0.0)
            pick[b, :, (s - first) * rows : (s - first + 1) * rows] = hit.astype(BF16)

    def place_step(s, carry):
        rank = jnp.broadcast_to(rank_row[s][0:1], (rows, rows)).T
        rank = jnp.concatenate([rank] * (routed // rows), axis=1)
        place[s] = jnp.where(token_lane == rank, 1.0, 0.0).astype(BF16)
        return carry

    lax.fori_loop(0, n_ctx, place_step, 0)

    def packed(all_ref, b):
        first, last = slots_of(b)
        source = all_ref[first:last]
        width = (last - first) * rows
        return dot(pick[b, :, 0:width], source.reshape(width, source.shape[2])).astype(BF16)

    def span(b, e=1):
        return slice(b * BLOCK, (b + e) * BLOCK)

    local[2].wait()
    local[3].wait()
    arrived(v_all.at[few], CH_K)
    arrived(v_all.at[few], CH_Q)
    for b in range(blocks):
        kq_c[span(b)] = packed(kq_all, b)
    for b in range(blocks):
        kt_c[:, span(b)] = kq_c[span(b), 0:HEAD].astype(F32).T.astype(BF16)

    key_at = lax.broadcasted_iota(jnp.int32, (BLOCK, BLOCK), 0)
    query_at = lax.broadcasted_iota(jnp.int32, (BLOCK, BLOCK), 1)
    causal = key_at <= query_at
    for i in range(blocks):
        q_i = kq_c[span(i), HEAD : 2 * HEAD]
        parts = [dot_nt(kq_c[span(j), 0:HEAD], q_i) for j in range(i + 1)]
        parts[i] = jnp.where(causal, parts[i], NEG_FILL)
        top = functools.reduce(jnp.maximum, [jnp.max(s, axis=0, keepdims=True) for s in parts])
        parts = [jnp.exp2((s - top) * (scale * LOG2E)) for s in parts]
        total = functools.reduce(jnp.add, [jnp.sum(e, axis=0, keepdims=True) for e in parts])
        inverse = 1.0 / total
        for j in range(i + 1):
            p_buf[span(j), span(i)] = (parts[j] * inverse).astype(BF16)

    arrived(d_all.at[few], CH_D)
    for b in range(blocks):
        d_c[span(b)] = packed(d_all, b)

    for j in range(blocks):
        rest = slice(j * BLOCK, routed)
        gv_c[span(j)] = dot(p_buf[span(j), rest], d_c[rest]).astype(BF16)

    def unpacked(m, source, low, high):
        begin = max(0, (m + 1) * BLOCK - BLOCK - routed)
        end = min(routed, (m + 1) * BLOCK)
        hits = place[m * per_block : (m + 1) * per_block].reshape(BLOCK, routed)
        return dot(hits[:, begin:end], source[begin:end, low:high])

    pairs = n_ctx // per_block
    for m in range(pairs):
        both = unpacked(m, gv_c, 0, HEAD).astype(BF16).reshape(per_block, rows, HEAD)
        gv_send[m * per_block : (m + 1) * per_block] = both

    to_peers(lambda p: gv_send.at[p], cols(gv_ref, me), CH_GV, GROUPS[0] + GROUPS[1])

    local[4].wait()
    arrived(v_all.at[few], CH_V)
    for b in range(blocks):
        v_c[span(b)] = packed(v_all, b)

    delta_slots = [jnp.zeros((8, rows), F32) for _ in range(n_ctx)]
    for i in range(blocks):
        d_i = d_c[span(i)]
        terms, weights = [], []
        for j in range(i + 1):
            p_ji = p_buf[span(j), span(i)].astype(F32)
            weights.append(p_ji)
            terms.append(p_ji * dot_nt(v_c[span(j)], d_i))
        delta = functools.reduce(jnp.add, [jnp.sum(t, axis=0, keepdims=True) for t in terms])
        for j in range(i + 1):
            ds_buf[span(j), span(i)] = (terms[j] - weights[j] * delta).astype(BF16)
        first, last = slots_of(i)
        width = (last - first) * rows
        moved = dot(three_rows(jnp.broadcast_to(delta, (8, BLOCK))), pick[i, :, 0:width])
        for s in range(first, last):
            delta_slots[s] = delta_slots[s] + moved[:, (s - first) * rows : (s - first + 1) * rows]
    for s in range(n_ctx):
        delta_send[s] = jnp.sum(delta_slots[s], axis=0, keepdims=True)
    delta_all[me] = delta_send[me]

    to_peers(lambda p: delta_send.at[p], delta_all.at[me], CH_DELTA)
    to_peers(lambda p: gv_send.at[p], cols(gv_ref, me), CH_GV, GROUPS[2])

    for j in range(blocks):
        rest = slice(j * BLOCK, routed)
        gkq_c[span(j), 0:HEAD] = (dot(ds_buf[span(j), rest], kq_c[rest, HEAD : 2 * HEAD]) * scale).astype(BF16)
    for i in range(blocks):
        upto = slice(0, (i + 1) * BLOCK)
        gkq_c[span(i), HEAD : 2 * HEAD] = (dot(kt_c[:, upto], ds_buf[upto, span(i)]) * scale).T.astype(BF16)
    for m in range(pairs):
        both = unpacked(m, gkq_c, 0, 2 * HEAD).astype(BF16)
        gk_send[m * per_block : (m + 1) * per_block] = both[:, 0:HEAD].reshape(per_block, rows, HEAD)
        gq_send[m * per_block : (m + 1) * per_block] = both[:, HEAD : 2 * HEAD].reshape(per_block, rows, HEAD)

    to_peers(lambda p: gk_send.at[p], cols(gk_ref, me), CH_GK, GROUPS[0] + GROUPS[1])

    arrived(delta_all.at[few], CH_DELTA)
    row_sum = delta_all[0]
    for h in range(1, n_ctx):
        row_sum += delta_all[h]
    row_sum = jnp.broadcast_to(row_sum, (8, rows))
    split = three_rows(row_sum * (1.0 - gate_row))
    for p in range(n_dp):
        term_send[p] = jnp.sum(dot(split, x_v[:, p * chunk : (p + 1) * chunk]), axis=0, keepdims=True)
    term_y[me_y] = term_send[own_y]
    for o in range(1, n_y):
        group = pl.ds(lax.rem(me_y + o, n_y) * n_z, n_z)
        remote(term_send.at[group], term_y.at[me_y], CH_TERM_Y, "dp", y_peer(o)).start()
    to_peers(lambda p: gk_send.at[p], cols(gk_ref, me), CH_GK, GROUPS[2])
    if n_y > 1:
        arrived(term_y.at[pl.ds(0, n_y - 1)], CH_TERM_Y)
    half = term_y[0]
    for p in range(1, n_y):
        half += term_y[p]
    term_half[...] = half
    term_z[me_z] = term_half[me_z]
    for o in range(1, n_z):
        remote(term_half.at[lax.rem(me_z + o, n_z)], term_z.at[me_z], CH_TERM_Z, "dp", z_peer(o)).start()
    to_peers(lambda p: gq_send.at[p], cols(gq_ref, me), CH_GQ, GROUPS[0] + GROUPS[1])
    if n_z > 1:
        arrived(term_z.at[pl.ds(0, n_z - 1)], CH_TERM_Z)
    term_sum = term_z[0]
    for p in range(1, n_z):
        term_sum += term_z[p]
    sum_send[...] = term_sum
    sum_all[me] = term_sum
    to_peers(lambda p: sum_send, sum_all.at[me], CH_SUM)
    to_peers(lambda p: gq_send.at[p], cols(gq_ref, me), CH_GQ, GROUPS[2])
    own = [
        pltpu.make_async_copy(gq_send.at[me], cols(gq_ref, me), local_sem.at[5]),
        pltpu.make_async_copy(gk_send.at[me], cols(gk_ref, me), local_sem.at[6]),
        pltpu.make_async_copy(gv_send.at[me], cols(gv_ref, me), local_sem.at[7]),
    ]
    for copy in own:
        copy.start()
    arrived(sum_all.at[few], CH_SUM)
    everything = sum_all[0]
    for c in range(1, n_ctx):
        everything += sum_all[c]
    rg_ref[...] = everything * (1.0 / total_routed)

    most = pl.ds(0, (n_ctx - 1) * HEAD)
    arrived(gv_ref.at[:, most], CH_GV)
    arrived(gk_ref.at[:, most], CH_GK)
    arrived(gq_ref.at[:, most], CH_GQ)
    for copy in own:
        copy.wait()
    for ref, channel in (
        (v_all, CH_K),
        (v_all, CH_Q),
        (v_all, CH_V),
        (d_all, CH_D),
        (live_all, CH_LIVE),
        (delta_all, CH_DELTA),
        (sum_all, CH_SUM),
        (gq_send, CH_GQ),
        (gk_send, CH_GK),
        (gv_send, CH_GV),
    ):
        sent(ref.at[few], channel)
    if n_z > 1:
        sent(w_all.at[pl.ds(0, n_z - 1)], CH_W_Z)
        sent(term_z.at[pl.ds(0, n_z - 1)], CH_TERM_Z)
    if n_y > 1:
        sent(w_all.at[pl.ds(0, (n_y - 1) * n_z)], CH_W_Y)
        sent(term_y.at[pl.ds(0, n_y - 1)], CH_TERM_Y)


def widen(gq_ref, gk_ref, gv_ref, rg_ref, q_out, k_out, v_out, r_out):
    q_out[...] = gq_ref[...].astype(F32)
    k_out[...] = gk_ref[...].astype(F32)
    v_out[...] = gv_ref[...].astype(F32)
    r_out[...] = rg_ref[0]


def body(route_pos, x_routed, w_router, queries, keys, values, d_gated):
    n_ctx = lax.axis_size("ctx")
    n_dp = lax.axis_size("dp")
    n_z = 4 if n_dp >= 16 else min(2, n_dp)
    n_y = n_dp // n_z
    rows, width = queries.shape[1:]
    routed = n_ctx * rows // 2
    blocks = routed // BLOCK
    chunk = w_router.shape[0]
    vmem = pl.BlockSpec(memory_space=pltpu.VMEM)
    hbm = pl.BlockSpec(memory_space=pltpu.HBM)
    heads = pltpu.VMEM((n_ctx, rows, HEAD), BF16)
    small = pltpu.VMEM((n_ctx, 1, rows), F32)
    compact = pltpu.VMEM((routed, HEAD), BF16)
    square = pltpu.VMEM((routed, routed), BF16)
    out = jax.ShapeDtypeStruct((rows, width), BF16)
    gq, gk, gv, rg = pl.pallas_call(
        functools.partial(kernel, n_ctx, n_y, n_z),
        out_shape=(out, out, out, jax.ShapeDtypeStruct((1, chunk), F32)),
        in_specs=[vmem, vmem] + [hbm] * 5,
        out_specs=(hbm, hbm, hbm, vmem),
        scratch_shapes=[
            pltpu.VMEM(x_routed.shape[1:], BF16),
            pltpu.VMEM((rows, width), F32),
            heads,
            pltpu.VMEM((n_ctx, rows, 2 * HEAD), BF16),
            heads,
            heads,
            small,
            pltpu.VMEM((1, rows), F32),
            pltpu.VMEM((n_dp, 1, chunk), BF16),
            pltpu.VMEM((n_ctx, 8, rows), F32),
            pltpu.VMEM((blocks, BLOCK, routed + BLOCK), BF16),
            pltpu.VMEM((n_ctx, rows, routed), BF16),
            pltpu.VMEM((routed, 2 * HEAD), BF16),
            pltpu.VMEM((HEAD, routed), BF16),
            compact,
            compact,
            square,
            square,
            pltpu.VMEM((routed, 2 * HEAD), BF16),
            compact,
            small,
            small,
            heads,
            heads,
            heads,
            pltpu.VMEM((n_dp, 1, chunk), F32),
            pltpu.VMEM((n_y, n_z, 1, chunk), F32),
            pltpu.VMEM((n_z, 1, chunk), F32),
            pltpu.VMEM((n_z, 1, chunk), F32),
            pltpu.VMEM((1, chunk), F32),
            pltpu.VMEM((n_ctx, 1, chunk), F32),
            pltpu.SemaphoreType.DMA((8,)),
            pltpu.SemaphoreType.DMA((CHANNELS,)),
            pltpu.SemaphoreType.DMA((CHANNELS,)),
        ],
        compiler_params=pltpu.CompilerParams(collective_id=0, has_side_effects=True, vmem_limit_bytes=60 * 1024 * 1024),
        name="routed_backward",
    )(route_pos, w_router, x_routed[0], queries[0], keys[0], values[0], d_gated[0])
    steps = 4
    tile = pl.BlockSpec((rows // steps, width), lambda i: (i, 0))
    wide = jax.ShapeDtypeStruct((rows, width), F32)
    gq, gk, gv, rg = pl.pallas_call(
        widen,
        grid=(steps,),
        out_shape=(wide, wide, wide, jax.ShapeDtypeStruct((chunk,), F32)),
        in_specs=[tile, tile, tile, pl.BlockSpec((1, chunk), lambda i: (0, 0))],
        out_specs=(tile, tile, tile, pl.BlockSpec((chunk,), lambda i: (0,))),
        name="widen",
    )(gq, gk, gv, rg)
    return (gq[None], gk[None], gv[None], rg)


def solution(mesh):
    placed = (
        P("dp", "ctx"),
        P("dp", "ctx", None),
        P("dp"),
        P("dp", "ctx", None),
        P("dp", "ctx", None),
        P("dp", "ctx", None),
        P("dp", "ctx", None),
    )
    return jax.shard_map(
        body,
        mesh=mesh,
        in_specs=placed,
        out_specs=(P("dp", "ctx", None), P("dp", "ctx", None), P("dp", "ctx", None), P("dp")),
        check_vma=False,
    )
```

```python
import functools

import jax
import jax.numpy as jnp
from jax import lax
from jax.experimental import pallas as pl
from jax.experimental.pallas import tpu as pltpu
from jax.sharding import PartitionSpec as P

HEAD = 128
NEG_FILL = -1e30
LOG2E = 1.4426950408889634
MESH = pl.DeviceIdType.MESH
F32 = jnp.float32
BF16 = jnp.bfloat16
BLOCK = 256
NT = (((1,), (1,)), ((), ()))
GROUPS = (
    ((1, 0, 0), (3, 0, 0), (0, 1, 0), (2, 1, 1), (2, 0, 0)),
    ((1, 0, 1), (3, 0, 1), (0, 1, 1), (2, 0, 1), (1, 1, 0)),
    ((3, 1, 0), (1, 1, 1), (3, 1, 1), (2, 1, 0), (0, 0, 1)),
)
EVERY = GROUPS[0] + GROUPS[1] + GROUPS[2]
CH_K, CH_Q, CH_V, CH_D, CH_LIVE, CH_W_Z, CH_W_Y, CH_DELTA, CH_TERM_Y, CH_TERM_Z, CH_SUM, CH_GQ, CH_GK, CH_GV = range(14)
CHANNELS = 14


def dot(a, b):
    return jnp.dot(a, b, preferred_element_type=F32)


def dot_nt(a, b):
    return lax.dot_general(a, b, NT, preferred_element_type=F32)


def three_rows(row):
    high = row.astype(BF16).astype(F32)
    middle = (row - high).astype(BF16).astype(F32)
    low = row - high - middle
    which = lax.broadcasted_iota(jnp.int32, row.shape, 0)
    split = jnp.where(which == 0, high, jnp.where(which == 1, middle, low))
    return jnp.where(which < 3, split, 0.0).astype(BF16)


def kernel(
    n_ctx,
    n_y,
    n_z,
    pos_ref,
    w_ref,
    x_hbm,
    q_hbm,
    k_hbm,
    v_hbm,
    d_hbm,
    gq_ref,
    gk_ref,
    gv_ref,
    rg_ref,
    x_v,
    d_v,
    d_send,
    kq_all,
    v_all,
    d_all,
    live_all,
    live_own,
    w_all,
    rank_row,
    pick,
    place,
    kq_c,
    kt_c,
    v_c,
    d_c,
    p_buf,
    ds_buf,
    gkq_c,
    gv_c,
    delta_send,
    delta_all,
    gq_send,
    gk_send,
    gv_send,
    term_send,
    term_y,
    term_half,
    term_z,
    sum_send,
    sum_all,
    local_sem,
    send_sem,
    recv_sem,
):
    me = lax.axis_index("ctx")
    me_dp = lax.axis_index("dp")
    n_dp = n_y * n_z
    me_y, me_z = me_dp // n_z, lax.rem(me_dp, n_z)
    rows = q_hbm.shape[0]
    slots = n_ctx * rows
    routed = slots // 2
    blocks = routed // BLOCK
    per_block = BLOCK // rows
    scale = HEAD ** (-0.5)
    chunk = w_all.shape[2]
    total_routed = float(n_dp * routed)

    def z_peer(o):
        return me_y * n_z + lax.rem(me_z + o, n_z)

    def y_peer(o):
        return lax.rem(me_y + o, n_y) * n_z + me_z

    barrier = pltpu.get_barrier_semaphore()
    for o in range(1, n_z):
        pl.semaphore_signal(barrier, inc=1, device_id={"dp": z_peer(o)}, device_id_type=MESH)
    for o in range(1, n_y):
        pl.semaphore_signal(barrier, inc=1, device_id={"dp": y_peer(o)}, device_id_type=MESH)
    for o in range(1, n_ctx):
        pl.semaphore_signal(barrier, inc=1, device_id={"ctx": lax.rem(me + o, n_ctx)}, device_id_type=MESH)

    def cols(ref, at):
        return ref.at[:, pl.ds(pl.multiple_of(at * HEAD, HEAD), HEAD)]

    local = [
        pltpu.make_async_copy(d_hbm, d_v, local_sem.at[0]),
        pltpu.make_async_copy(x_hbm, x_v, local_sem.at[1]),
        pltpu.make_async_copy(cols(k_hbm, me), kq_all.at[me, :, pl.ds(0, HEAD)], local_sem.at[2]),
        pltpu.make_async_copy(cols(q_hbm, me), kq_all.at[me, :, pl.ds(HEAD, HEAD)], local_sem.at[3]),
        pltpu.make_async_copy(cols(v_hbm, me), v_all.at[me], local_sem.at[4]),
    ]
    for copy in local:
        copy.start()

    def remote(src, dst, channel, axis, peer):
        return pltpu.make_async_remote_copy(
            src_ref=src,
            dst_ref=dst,
            send_sem=send_sem.at[channel],
            recv_sem=recv_sem.at[channel],
            device_id={axis: peer},
            device_id_type=MESH,
        )

    def to_peers(source_of, dst, channel, group=EVERY):
        for dx, dz, dc in group:
            peer = 4 * lax.rem(me // 4 + dx, n_ctx // 4) + 2 * lax.rem(me // 2 + dz, 2) + lax.rem(me + dc, 2)
            remote(source_of(peer), dst, channel, "ctx", peer).start()

    def arrived(ref, channel):
        remote(ref, ref, channel, "ctx", lax.rem(me + 1, n_ctx)).wait_recv()

    def sent(ref, channel):
        remote(ref, ref, channel, "ctx", lax.rem(me + 1, n_ctx)).wait_send()

    few = pl.ds(0, n_ctx - 1)

    live_row = jnp.where(jnp.broadcast_to(pos_ref[...], (8, rows)) >= 0, 1.0, 0.0).astype(F32)
    live_own[...] = live_row[0:1]
    live_all[me] = live_row[0:1]
    w_all[me_dp] = w_ref[...].reshape(1, chunk)

    pl.semaphore_wait(barrier, n_ctx + n_y + n_z - 3)

    for o in range(1, n_z):
        remote(w_all.at[me_dp], w_all.at[me_dp], CH_W_Z, "dp", z_peer(o)).start()
    to_peers(lambda p: live_own, live_all.at[me], CH_LIVE)
    to_peers(lambda p: cols(k_hbm, p), kq_all.at[me, :, pl.ds(0, HEAD)], CH_K)
    to_peers(lambda p: cols(q_hbm, p), kq_all.at[me, :, pl.ds(HEAD, HEAD)], CH_Q)
    to_peers(lambda p: cols(v_hbm, p), v_all.at[me], CH_V, GROUPS[0])

    local[1].wait()
    if n_z > 1:
        arrived(w_all.at[pl.ds(0, n_z - 1)], CH_W_Z)
    own_y = pl.ds(me_y * n_z, n_z)
    for o in range(1, n_y):
        remote(w_all.at[own_y], w_all.at[own_y], CH_W_Y, "dp", y_peer(o)).start()
    if n_y > 1:
        arrived(w_all.at[pl.ds(0, (n_y - 1) * n_z)], CH_W_Y)
    logit = jnp.zeros((rows, rows), F32)
    for p in range(n_dp):
        w_p = jnp.broadcast_to(w_all[p].astype(F32), (rows, chunk)).astype(BF16)
        logit += dot_nt(x_v[:, p * chunk : (p + 1) * chunk], w_p)
    gate = jax.nn.sigmoid(logit)
    gate_row = gate.T[0:8]
    factor = gate * jnp.broadcast_to(live_row[0:1], (rows, rows)).T
    local[0].wait()
    for h in range(n_ctx):
        d_send[h] = (d_v[:, h * HEAD : (h + 1) * HEAD] * factor).astype(BF16)
    d_all[me] = d_send[me]

    arrived(live_all.at[few], CH_LIVE)
    lane = lax.broadcasted_iota(jnp.int32, (8, rows), 1).astype(F32)
    before = jnp.zeros((8, rows), F32)
    for s in range(n_ctx):
        live_s = jnp.broadcast_to(live_all[s], (8, rows))
        rank_row[s] = jnp.where(live_s > 0.0, before + lane, -1.0)
        before = before + jnp.sum(live_s, axis=1, keepdims=True)

    to_peers(lambda p: d_send.at[p], d_all.at[me], CH_D)
    to_peers(lambda p: cols(v_hbm, p), v_all.at[me], CH_V, GROUPS[1] + GROUPS[2])

    token_row = lax.broadcasted_iota(jnp.int32, (BLOCK, rows), 0).astype(F32)
    token_lane = lax.broadcasted_iota(jnp.int32, (rows, routed), 1).astype(F32)

    def slots_of(b):
        first = b * per_block
        return first, min(n_ctx, first + (routed + BLOCK) // rows)

    for b in range(blocks):
        first, last = slots_of(b)
        for s in range(first, last):
            rank = jnp.broadcast_to(rank_row[s][0:1], (BLOCK, rows))
            hit = jnp.where(token_row + float(b * BLOCK) == rank, 1.0, 0.0)
            pick[b, :, (s - first) * rows : (s - first + 1) * rows] = hit.astype(BF16)

    def place_step(s, carry):
        rank = jnp.broadcast_to(rank_row[s][0:1], (rows, rows)).T
        rank = jnp.concatenate([rank] * (routed // rows), axis=1)
        place[s] = jnp.where(token_lane == rank, 1.0, 0.0).astype(BF16)
        return carry

    lax.fori_loop(0, n_ctx, place_step, 0)

    def packed(all_ref, b):
        first, last = slots_of(b)
        source = all_ref[first:last]
        width = (last - first) * rows
        return dot(pick[b, :, 0:width], source.reshape(width, source.shape[2])).astype(BF16)

    def span(b, e=1):
        return slice(b * BLOCK, (b + e) * BLOCK)

    local[2].wait()
    local[3].wait()
    arrived(v_all.at[few], CH_K)
    arrived(v_all.at[few], CH_Q)
    for b in range(blocks):
        kq_c[span(b)] = packed(kq_all, b)
    for b in range(blocks):
        kt_c[:, span(b)] = kq_c[span(b), 0:HEAD].astype(F32).T.astype(BF16)

    key_at = lax.broadcasted_iota(jnp.int32, (BLOCK, BLOCK), 0)
    query_at = lax.broadcasted_iota(jnp.int32, (BLOCK, BLOCK), 1)
    causal = key_at <= query_at
    for i in range(blocks):
        q_i = kq_c[span(i), HEAD : 2 * HEAD]
        parts = [dot_nt(kq_c[span(j), 0:HEAD], q_i) for j in range(i + 1)]
        parts[i] = jnp.where(causal, parts[i], NEG_FILL)
        top = functools.reduce(jnp.maximum, [jnp.max(s, axis=0, keepdims=True) for s in parts])
        parts = [jnp.exp2((s - top) * (scale * LOG2E)) for s in parts]
        total = functools.reduce(jnp.add, [jnp.sum(e, axis=0, keepdims=True) for e in parts])
        inverse = 1.0 / total
        for j in range(i + 1):
            p_buf[span(j), span(i)] = (parts[j] * inverse).astype(BF16)

    arrived(d_all.at[few], CH_D)
    for b in range(blocks):
        d_c[span(b)] = packed(d_all, b)

    for j in range(blocks):
        rest = slice(j * BLOCK, routed)
        gv_c[span(j)] = dot(p_buf[span(j), rest], d_c[rest]).astype(BF16)

    def unpacked(m, source, low, high):
        begin = max(0, (m + 1) * BLOCK - BLOCK - routed)
        end = min(routed, (m + 1) * BLOCK)
        hits = place[m * per_block : (m + 1) * per_block].reshape(BLOCK, routed)
        return dot(hits[:, begin:end], source[begin:end, low:high])

    pairs = n_ctx // per_block
    for m in range(pairs):
        both = unpacked(m, gv_c, 0, HEAD).astype(BF16).reshape(per_block, rows, HEAD)
        gv_send[m * per_block : (m + 1) * per_block] = both

    to_peers(lambda p: gv_send.at[p], cols(gv_ref, me), CH_GV, GROUPS[0] + GROUPS[1])

    local[4].wait()
    arrived(v_all.at[few], CH_V)
    for b in range(blocks):
        v_c[span(b)] = packed(v_all, b)

    delta_slots = [jnp.zeros((8, rows), F32) for _ in range(n_ctx)]
    for i in range(blocks):
        d_i = d_c[span(i)]
        terms, weights = [], []
        for j in range(i + 1):
            p_ji = p_buf[span(j), span(i)].astype(F32)
            weights.append(p_ji)
            terms.append(p_ji * dot_nt(v_c[span(j)], d_i))
        delta = functools.reduce(jnp.add, [jnp.sum(t, axis=0, keepdims=True) for t in terms])
        for j in range(i + 1):
            ds_buf[span(j), span(i)] = (terms[j] - weights[j] * delta).astype(BF16)
        first, last = slots_of(i)
        width = (last - first) * rows
        moved = dot(three_rows(jnp.broadcast_to(delta, (8, BLOCK))), pick[i, :, 0:width])
        for s in range(first, last):
            delta_slots[s] = delta_slots[s] + moved[:, (s - first) * rows : (s - first + 1) * rows]
    for s in range(n_ctx):
        delta_send[s] = jnp.sum(delta_slots[s], axis=0, keepdims=True)
    delta_all[me] = delta_send[me]

    to_peers(lambda p: delta_send.at[p], delta_all.at[me], CH_DELTA)
    to_peers(lambda p: gv_send.at[p], cols(gv_ref, me), CH_GV, GROUPS[2])

    for j in range(blocks):
        rest = slice(j * BLOCK, routed)
        gkq_c[span(j), 0:HEAD] = (dot(ds_buf[span(j), rest], kq_c[rest, HEAD : 2 * HEAD]) * scale).astype(BF16)
    for i in range(blocks):
        upto = slice(0, (i + 1) * BLOCK)
        gkq_c[span(i), HEAD : 2 * HEAD] = (dot(kt_c[:, upto], ds_buf[upto, span(i)]) * scale).T.astype(BF16)
    for m in range(pairs):
        both = unpacked(m, gkq_c, 0, 2 * HEAD).astype(BF16)
        gk_send[m * per_block : (m + 1) * per_block] = both[:, 0:HEAD].reshape(per_block, rows, HEAD)
        gq_send[m * per_block : (m + 1) * per_block] = both[:, HEAD : 2 * HEAD].reshape(per_block, rows, HEAD)

    to_peers(lambda p: gk_send.at[p], cols(gk_ref, me), CH_GK, GROUPS[0] + GROUPS[1])

    arrived(delta_all.at[few], CH_DELTA)
    row_sum = delta_all[0]
    for h in range(1, n_ctx):
        row_sum += delta_all[h]
    row_sum = jnp.broadcast_to(row_sum, (8, rows))
    split = three_rows(row_sum * (1.0 - gate_row))
    for p in range(n_dp):
        term_send[p] = jnp.sum(dot(split, x_v[:, p * chunk : (p + 1) * chunk]), axis=0, keepdims=True)
    term_y[me_y] = term_send[own_y]
    for o in range(1, n_y):
        group = pl.ds(lax.rem(me_y + o, n_y) * n_z, n_z)
        remote(term_send.at[group], term_y.at[me_y], CH_TERM_Y, "dp", y_peer(o)).start()
    to_peers(lambda p: gk_send.at[p], cols(gk_ref, me), CH_GK, GROUPS[2])
    if n_y > 1:
        arrived(term_y.at[pl.ds(0, n_y - 1)], CH_TERM_Y)
    half = term_y[0]
    for p in range(1, n_y):
        half += term_y[p]
    term_half[...] = half
    term_z[me_z] = term_half[me_z]
    for o in range(1, n_z):
        remote(term_half.at[lax.rem(me_z + o, n_z)], term_z.at[me_z], CH_TERM_Z, "dp", z_peer(o)).start()
    to_peers(lambda p: gq_send.at[p], cols(gq_ref, me), CH_GQ, GROUPS[0] + GROUPS[1])
    if n_z > 1:
        arrived(term_z.at[pl.ds(0, n_z - 1)], CH_TERM_Z)
    term_sum = term_z[0]
    for p in range(1, n_z):
        term_sum += term_z[p]
    sum_send[...] = term_sum
    sum_all[me] = term_sum
    to_peers(lambda p: sum_send, sum_all.at[me], CH_SUM)
    to_peers(lambda p: gq_send.at[p], cols(gq_ref, me), CH_GQ, GROUPS[2])
    own = [
        pltpu.make_async_copy(gq_send.at[me], cols(gq_ref, me), local_sem.at[5]),
        pltpu.make_async_copy(gk_send.at[me], cols(gk_ref, me), local_sem.at[6]),
        pltpu.make_async_copy(gv_send.at[me], cols(gv_ref, me), local_sem.at[7]),
    ]
    for copy in own:
        copy.start()
    arrived(sum_all.at[few], CH_SUM)
    everything = sum_all[0]
    for c in range(1, n_ctx):
        everything += sum_all[c]
    rg_ref[...] = everything * (1.0 / total_routed)

    most = pl.ds(0, (n_ctx - 1) * HEAD)
    arrived(gv_ref.at[:, most], CH_GV)
    arrived(gk_ref.at[:, most], CH_GK)
    arrived(gq_ref.at[:, most], CH_GQ)
    for copy in own:
        copy.wait()
    for ref, channel in (
        (v_all, CH_K),
        (v_all, CH_Q),
        (v_all, CH_V),
        (d_all, CH_D),
        (live_all, CH_LIVE),
        (delta_all, CH_DELTA),
        (sum_all, CH_SUM),
        (gq_send, CH_GQ),
        (gk_send, CH_GK),
        (gv_send, CH_GV),
    ):
        sent(ref.at[few], channel)
    if n_z > 1:
        sent(w_all.at[pl.ds(0, n_z - 1)], CH_W_Z)
        sent(term_z.at[pl.ds(0, n_z - 1)], CH_TERM_Z)
    if n_y > 1:
        sent(w_all.at[pl.ds(0, (n_y - 1) * n_z)], CH_W_Y)
        sent(term_y.at[pl.ds(0, n_y - 1)], CH_TERM_Y)


def widen(gq_ref, gk_ref, gv_ref, rg_ref, q_out, k_out, v_out, r_out):
    q_out[...] = gq_ref[...].astype(F32)
    k_out[...] = gk_ref[...].astype(F32)
    v_out[...] = gv_ref[...].astype(F32)
    r_out[...] = rg_ref[0]


def body(route_pos, x_routed, w_router, queries, keys, values, d_gated):
    n_ctx = lax.axis_size("ctx")
    n_dp = lax.axis_size("dp")
    n_z = 4 if n_dp >= 16 else min(2, n_dp)
    n_y = n_dp // n_z
    rows, width = queries.shape[1:]
    routed = n_ctx * rows // 2
    blocks = routed // BLOCK
    chunk = w_router.shape[0]
    vmem = pl.BlockSpec(memory_space=pltpu.VMEM)
    hbm = pl.BlockSpec(memory_space=pltpu.HBM)
    heads = pltpu.VMEM((n_ctx, rows, HEAD), BF16)
    small = pltpu.VMEM((n_ctx, 1, rows), F32)
    compact = pltpu.VMEM((routed, HEAD), BF16)
    square = pltpu.VMEM((routed, routed), BF16)
    out = jax.ShapeDtypeStruct((rows, width), BF16)
    gq, gk, gv, rg = pl.pallas_call(
        functools.partial(kernel, n_ctx, n_y, n_z),
        out_shape=(out, out, out, jax.ShapeDtypeStruct((1, chunk), F32)),
        in_specs=[vmem, vmem] + [hbm] * 5,
        out_specs=(hbm, hbm, hbm, vmem),
        scratch_shapes=[
            pltpu.VMEM(x_routed.shape[1:], BF16),
            pltpu.VMEM((rows, width), F32),
            heads,
            pltpu.VMEM((n_ctx, rows, 2 * HEAD), BF16),
            heads,
            heads,
            small,
            pltpu.VMEM((1, rows), F32),
            pltpu.VMEM((n_dp, 1, chunk), BF16),
            pltpu.VMEM((n_ctx, 8, rows), F32),
            pltpu.VMEM((blocks, BLOCK, routed + BLOCK), BF16),
            pltpu.VMEM((n_ctx, rows, routed), BF16),
            pltpu.VMEM((routed, 2 * HEAD), BF16),
            pltpu.VMEM((HEAD, routed), BF16),
            compact,
            compact,
            square,
            square,
            pltpu.VMEM((routed, 2 * HEAD), BF16),
            compact,
            small,
            small,
            heads,
            heads,
            heads,
            pltpu.VMEM((n_dp, 1, chunk), F32),
            pltpu.VMEM((n_y, n_z, 1, chunk), F32),
            pltpu.VMEM((n_z, 1, chunk), F32),
            pltpu.VMEM((n_z, 1, chunk), F32),
            pltpu.VMEM((1, chunk), F32),
            pltpu.VMEM((n_ctx, 1, chunk), F32),
            pltpu.SemaphoreType.DMA((8,)),
            pltpu.SemaphoreType.DMA((CHANNELS,)),
            pltpu.SemaphoreType.DMA((CHANNELS,)),
        ],
        compiler_params=pltpu.CompilerParams(collective_id=0, has_side_effects=True, vmem_limit_bytes=60 * 1024 * 1024),
        name="routed_backward",
    )(route_pos, w_router, x_routed[0], queries[0], keys[0], values[0], d_gated[0])
    steps = 2
    tile = pl.BlockSpec((rows // steps, width), lambda i: (i, 0))
    wide = jax.ShapeDtypeStruct((rows, width), F32)
    gq, gk, gv, rg = pl.pallas_call(
        widen,
        grid=(steps,),
        out_shape=(wide, wide, wide, jax.ShapeDtypeStruct((chunk,), F32)),
        in_specs=[tile, tile, tile, pl.BlockSpec((1, chunk), lambda i: (0, 0))],
        out_specs=(tile, tile, tile, pl.BlockSpec((chunk,), lambda i: (0,))),
        name="widen",
    )(gq, gk, gv, rg)
    return (gq[None], gk[None], gv[None], rg)


def solution(mesh):
    placed = (
        P("dp", "ctx"),
        P("dp", "ctx", None),
        P("dp"),
        P("dp", "ctx", None),
        P("dp", "ctx", None),
        P("dp", "ctx", None),
        P("dp", "ctx", None),
    )
    return jax.shard_map(
        body,
        mesh=mesh,
        in_specs=placed,
        out_specs=(P("dp", "ctx", None), P("dp", "ctx", None), P("dp", "ctx", None), P("dp")),
        check_vma=False,
    )
```

```python
import functools

import jax
import jax.numpy as jnp
from jax import lax
from jax.experimental import pallas as pl
from jax.experimental.pallas import tpu as pltpu
from jax.sharding import PartitionSpec as P

HEAD = 128
NEG_FILL = -1e30
LOG2E = 1.4426950408889634
MESH = pl.DeviceIdType.MESH
F32 = jnp.float32
BF16 = jnp.bfloat16
BLOCK = 256
NT = (((1,), (1,)), ((), ()))
GROUPS = (
    ((2, 0, 0), (3, 1, 1), (1, 1, 0), (2, 1, 0), (0, 0, 1)),
    ((2, 1, 1), (1, 0, 0), (3, 0, 0), (0, 1, 0), (1, 1, 1)),
    ((2, 0, 1), (1, 0, 1), (3, 0, 1), (0, 1, 1), (3, 1, 0)),
)
EVERY = GROUPS[0] + GROUPS[1] + GROUPS[2]
CH_K, CH_Q, CH_V, CH_D, CH_LIVE, CH_W_Z, CH_W_Y, CH_DELTA, CH_TERM_Y, CH_TERM_Z, CH_SUM, CH_GQ, CH_GK, CH_GV = range(14)
CHANNELS = 14


def dot(a, b):
    return jnp.dot(a, b, preferred_element_type=F32)


def dot_nt(a, b):
    return lax.dot_general(a, b, NT, preferred_element_type=F32)


def three_rows(row):
    high = row.astype(BF16).astype(F32)
    middle = (row - high).astype(BF16).astype(F32)
    low = row - high - middle
    which = lax.broadcasted_iota(jnp.int32, row.shape, 0)
    split = jnp.where(which == 0, high, jnp.where(which == 1, middle, low))
    return jnp.where(which < 3, split, 0.0).astype(BF16)


def kernel(
    n_ctx,
    n_y,
    n_z,
    pos_ref,
    w_ref,
    x_hbm,
    q_hbm,
    k_hbm,
    v_hbm,
    d_hbm,
    gq_ref,
    gk_ref,
    gv_ref,
    rg_ref,
    x_v,
    d_v,
    d_send,
    kq_all,
    v_all,
    d_all,
    live_all,
    live_own,
    w_all,
    rank_row,
    pick,
    place,
    kq_c,
    kt_c,
    v_c,
    d_c,
    p_buf,
    ds_buf,
    gkq_c,
    gv_c,
    delta_send,
    delta_all,
    gq_send,
    gk_send,
    gv_send,
    term_send,
    term_y,
    term_half,
    term_z,
    sum_send,
    sum_all,
    local_sem,
    send_sem,
    recv_sem,
):
    me = lax.axis_index("ctx")
    me_dp = lax.axis_index("dp")
    n_dp = n_y * n_z
    me_y, me_z = me_dp // n_z, lax.rem(me_dp, n_z)
    rows = q_hbm.shape[0]
    slots = n_ctx * rows
    routed = slots // 2
    blocks = routed // BLOCK
    per_block = BLOCK // rows
    scale = HEAD ** (-0.5)
    chunk = w_all.shape[2]
    total_routed = float(n_dp * routed)

    def z_peer(o):
        return me_y * n_z + lax.rem(me_z + o, n_z)

    def y_peer(o):
        return lax.rem(me_y + o, n_y) * n_z + me_z

    barrier = pltpu.get_barrier_semaphore()
    for o in range(1, n_z):
        pl.semaphore_signal(barrier, inc=1, device_id={"dp": z_peer(o)}, device_id_type=MESH)
    for o in range(1, n_y):
        pl.semaphore_signal(barrier, inc=1, device_id={"dp": y_peer(o)}, device_id_type=MESH)
    for o in range(1, n_ctx):
        pl.semaphore_signal(barrier, inc=1, device_id={"ctx": lax.rem(me + o, n_ctx)}, device_id_type=MESH)

    def cols(ref, at):
        return ref.at[:, pl.ds(pl.multiple_of(at * HEAD, HEAD), HEAD)]

    local = [
        pltpu.make_async_copy(d_hbm, d_v, local_sem.at[0]),
        pltpu.make_async_copy(x_hbm, x_v, local_sem.at[1]),
        pltpu.make_async_copy(cols(k_hbm, me), kq_all.at[me, :, pl.ds(0, HEAD)], local_sem.at[2]),
        pltpu.make_async_copy(cols(q_hbm, me), kq_all.at[me, :, pl.ds(HEAD, HEAD)], local_sem.at[3]),
        pltpu.make_async_copy(cols(v_hbm, me), v_all.at[me], local_sem.at[4]),
    ]
    for copy in local:
        copy.start()

    def remote(src, dst, channel, axis, peer):
        return pltpu.make_async_remote_copy(
            src_ref=src,
            dst_ref=dst,
            send_sem=send_sem.at[channel],
            recv_sem=recv_sem.at[channel],
            device_id={axis: peer},
            device_id_type=MESH,
        )

    def to_peers(source_of, dst, channel, group=EVERY):
        for dx, dz, dc in group:
            peer = 4 * lax.rem(me // 4 + dx, n_ctx // 4) + 2 * lax.rem(me // 2 + dz, 2) + lax.rem(me + dc, 2)
            remote(source_of(peer), dst, channel, "ctx", peer).start()

    def arrived(ref, channel):
        remote(ref, ref, channel, "ctx", lax.rem(me + 1, n_ctx)).wait_recv()

    def sent(ref, channel):
        remote(ref, ref, channel, "ctx", lax.rem(me + 1, n_ctx)).wait_send()

    few = pl.ds(0, n_ctx - 1)

    live_row = jnp.where(jnp.broadcast_to(pos_ref[...], (8, rows)) >= 0, 1.0, 0.0).astype(F32)
    live_own[...] = live_row[0:1]
    live_all[me] = live_row[0:1]
    w_all[me_dp] = w_ref[...].reshape(1, chunk)

    pl.semaphore_wait(barrier, n_ctx + n_y + n_z - 3)

    for o in range(1, n_z):
        remote(w_all.at[me_dp], w_all.at[me_dp], CH_W_Z, "dp", z_peer(o)).start()
    to_peers(lambda p: live_own, live_all.at[me], CH_LIVE)
    to_peers(lambda p: cols(k_hbm, p), kq_all.at[me, :, pl.ds(0, HEAD)], CH_K)
    to_peers(lambda p: cols(q_hbm, p), kq_all.at[me, :, pl.ds(HEAD, HEAD)], CH_Q)
    to_peers(lambda p: cols(v_hbm, p), v_all.at[me], CH_V, GROUPS[0])

    local[1].wait()
    if n_z > 1:
        arrived(w_all.at[pl.ds(0, n_z - 1)], CH_W_Z)
    own_y = pl.ds(me_y * n_z, n_z)
    for o in range(1, n_y):
        remote(w_all.at[own_y], w_all.at[own_y], CH_W_Y, "dp", y_peer(o)).start()
    if n_y > 1:
        arrived(w_all.at[pl.ds(0, (n_y - 1) * n_z)], CH_W_Y)
    logit = jnp.zeros((rows, rows), F32)
    for p in range(n_dp):
        w_p = jnp.broadcast_to(w_all[p].astype(F32), (rows, chunk)).astype(BF16)
        logit += dot_nt(x_v[:, p * chunk : (p + 1) * chunk], w_p)
    gate = jax.nn.sigmoid(logit)
    gate_row = gate.T[0:8]
    factor = gate * jnp.broadcast_to(live_row[0:1], (rows, rows)).T
    local[0].wait()
    for h in range(n_ctx):
        d_send[h] = (d_v[:, h * HEAD : (h + 1) * HEAD] * factor).astype(BF16)
    d_all[me] = d_send[me]

    arrived(live_all.at[few], CH_LIVE)
    lane = lax.broadcasted_iota(jnp.int32, (8, rows), 1).astype(F32)
    before = jnp.zeros((8, rows), F32)
    for s in range(n_ctx):
        live_s = jnp.broadcast_to(live_all[s], (8, rows))
        rank_row[s] = jnp.where(live_s > 0.0, before + lane, -1.0)
        before = before + jnp.sum(live_s, axis=1, keepdims=True)

    to_peers(lambda p: d_send.at[p], d_all.at[me], CH_D)
    to_peers(lambda p: cols(v_hbm, p), v_all.at[me], CH_V, GROUPS[1] + GROUPS[2])

    token_row = lax.broadcasted_iota(jnp.int32, (BLOCK, rows), 0).astype(F32)
    token_lane = lax.broadcasted_iota(jnp.int32, (rows, routed), 1).astype(F32)

    def slots_of(b):
        first = b * per_block
        return first, min(n_ctx, first + (routed + BLOCK) // rows)

    for b in range(blocks):
        first, last = slots_of(b)
        for s in range(first, last):
            rank = jnp.broadcast_to(rank_row[s][0:1], (BLOCK, rows))
            hit = jnp.where(token_row + float(b * BLOCK) == rank, 1.0, 0.0)
            pick[b, :, (s - first) * rows : (s - first + 1) * rows] = hit.astype(BF16)

    def place_step(s, carry):
        rank = jnp.broadcast_to(rank_row[s][0:1], (rows, rows)).T
        rank = jnp.concatenate([rank] * (routed // rows), axis=1)
        place[s] = jnp.where(token_lane == rank, 1.0, 0.0).astype(BF16)
        return carry

    lax.fori_loop(0, n_ctx, place_step, 0)

    def packed(all_ref, b):
        first, last = slots_of(b)
        source = all_ref[first:last]
        width = (last - first) * rows
        return dot(pick[b, :, 0:width], source.reshape(width, source.shape[2])).astype(BF16)

    def span(b, e=1):
        return slice(b * BLOCK, (b + e) * BLOCK)

    local[2].wait()
    local[3].wait()
    arrived(v_all.at[few], CH_K)
    arrived(v_all.at[few], CH_Q)
    for b in range(blocks):
        kq_c[span(b)] = packed(kq_all, b)
    for b in range(blocks):
        kt_c[:, span(b)] = kq_c[span(b), 0:HEAD].astype(F32).T.astype(BF16)

    key_at = lax.broadcasted_iota(jnp.int32, (BLOCK, BLOCK), 0)
    query_at = lax.broadcasted_iota(jnp.int32, (BLOCK, BLOCK), 1)
    causal = key_at <= query_at
    for i in range(blocks):
        q_i = kq_c[span(i), HEAD : 2 * HEAD]
        parts = [dot_nt(kq_c[span(j), 0:HEAD], q_i) for j in range(i + 1)]
        parts[i] = jnp.where(causal, parts[i], NEG_FILL)
        top = functools.reduce(jnp.maximum, [jnp.max(s, axis=0, keepdims=True) for s in parts])
        parts = [jnp.exp2((s - top) * (scale * LOG2E)) for s in parts]
        total = functools.reduce(jnp.add, [jnp.sum(e, axis=0, keepdims=True) for e in parts])
        inverse = 1.0 / total
        for j in range(i + 1):
            p_buf[span(j), span(i)] = (parts[j] * inverse).astype(BF16)

    arrived(d_all.at[few], CH_D)
    for b in range(blocks):
        d_c[span(b)] = packed(d_all, b)

    for j in range(blocks):
        rest = slice(j * BLOCK, routed)
        gv_c[span(j)] = dot(p_buf[span(j), rest], d_c[rest]).astype(BF16)

    def unpacked(m, source, low, high):
        begin = max(0, (m + 1) * BLOCK - BLOCK - routed)
        end = min(routed, (m + 1) * BLOCK)
        hits = place[m * per_block : (m + 1) * per_block].reshape(BLOCK, routed)
        return dot(hits[:, begin:end], source[begin:end, low:high])

    pairs = n_ctx // per_block
    for m in range(pairs):
        both = unpacked(m, gv_c, 0, HEAD).astype(BF16).reshape(per_block, rows, HEAD)
        gv_send[m * per_block : (m + 1) * per_block] = both

    to_peers(lambda p: gv_send.at[p], cols(gv_ref, me), CH_GV, GROUPS[0] + GROUPS[1])

    local[4].wait()
    arrived(v_all.at[few], CH_V)
    for b in range(blocks):
        v_c[span(b)] = packed(v_all, b)

    delta_slots = [jnp.zeros((8, rows), F32) for _ in range(n_ctx)]
    for i in range(blocks):
        d_i = d_c[span(i)]
        terms, weights = [], []
        for j in range(i + 1):
            p_ji = p_buf[span(j), span(i)].astype(F32)
            weights.append(p_ji)
            terms.append(p_ji * dot_nt(v_c[span(j)], d_i))
        delta = functools.reduce(jnp.add, [jnp.sum(t, axis=0, keepdims=True) for t in terms])
        for j in range(i + 1):
            ds_buf[span(j), span(i)] = (terms[j] - weights[j] * delta).astype(BF16)
        first, last = slots_of(i)
        width = (last - first) * rows
        moved = dot(three_rows(jnp.broadcast_to(delta, (8, BLOCK))), pick[i, :, 0:width])
        for s in range(first, last):
            delta_slots[s] = delta_slots[s] + moved[:, (s - first) * rows : (s - first + 1) * rows]
    for s in range(n_ctx):
        delta_send[s] = jnp.sum(delta_slots[s], axis=0, keepdims=True)
    delta_all[me] = delta_send[me]

    to_peers(lambda p: delta_send.at[p], delta_all.at[me], CH_DELTA)
    to_peers(lambda p: gv_send.at[p], cols(gv_ref, me), CH_GV, GROUPS[2])

    for j in range(blocks):
        rest = slice(j * BLOCK, routed)
        gkq_c[span(j), 0:HEAD] = (dot(ds_buf[span(j), rest], kq_c[rest, HEAD : 2 * HEAD]) * scale).astype(BF16)
    for i in range(blocks):
        upto = slice(0, (i + 1) * BLOCK)
        gkq_c[span(i), HEAD : 2 * HEAD] = (dot(kt_c[:, upto], ds_buf[upto, span(i)]) * scale).T.astype(BF16)
    for m in range(pairs):
        both = unpacked(m, gkq_c, 0, 2 * HEAD).astype(BF16)
        gk_send[m * per_block : (m + 1) * per_block] = both[:, 0:HEAD].reshape(per_block, rows, HEAD)
        gq_send[m * per_block : (m + 1) * per_block] = both[:, HEAD : 2 * HEAD].reshape(per_block, rows, HEAD)

    to_peers(lambda p: gk_send.at[p], cols(gk_ref, me), CH_GK, GROUPS[0] + GROUPS[1])

    arrived(delta_all.at[few], CH_DELTA)
    row_sum = delta_all[0]
    for h in range(1, n_ctx):
        row_sum += delta_all[h]
    row_sum = jnp.broadcast_to(row_sum, (8, rows))
    split = three_rows(row_sum * (1.0 - gate_row))
    for p in range(n_dp):
        term_send[p] = jnp.sum(dot(split, x_v[:, p * chunk : (p + 1) * chunk]), axis=0, keepdims=True)
    term_y[me_y] = term_send[own_y]
    for o in range(1, n_y):
        group = pl.ds(lax.rem(me_y + o, n_y) * n_z, n_z)
        remote(term_send.at[group], term_y.at[me_y], CH_TERM_Y, "dp", y_peer(o)).start()
    to_peers(lambda p: gk_send.at[p], cols(gk_ref, me), CH_GK, GROUPS[2])
    if n_y > 1:
        arrived(term_y.at[pl.ds(0, n_y - 1)], CH_TERM_Y)
    half = term_y[0]
    for p in range(1, n_y):
        half += term_y[p]
    term_half[...] = half
    term_z[me_z] = term_half[me_z]
    for o in range(1, n_z):
        remote(term_half.at[lax.rem(me_z + o, n_z)], term_z.at[me_z], CH_TERM_Z, "dp", z_peer(o)).start()
    to_peers(lambda p: gq_send.at[p], cols(gq_ref, me), CH_GQ, GROUPS[0] + GROUPS[1])
    if n_z > 1:
        arrived(term_z.at[pl.ds(0, n_z - 1)], CH_TERM_Z)
    term_sum = term_z[0]
    for p in range(1, n_z):
        term_sum += term_z[p]
    sum_send[...] = term_sum
    sum_all[me] = term_sum
    to_peers(lambda p: sum_send, sum_all.at[me], CH_SUM)
    to_peers(lambda p: gq_send.at[p], cols(gq_ref, me), CH_GQ, GROUPS[2])
    own = [
        pltpu.make_async_copy(gq_send.at[me], cols(gq_ref, me), local_sem.at[5]),
        pltpu.make_async_copy(gk_send.at[me], cols(gk_ref, me), local_sem.at[6]),
        pltpu.make_async_copy(gv_send.at[me], cols(gv_ref, me), local_sem.at[7]),
    ]
    for copy in own:
        copy.start()
    arrived(sum_all.at[few], CH_SUM)
    everything = sum_all[0]
    for c in range(1, n_ctx):
        everything += sum_all[c]
    rg_ref[...] = everything * (1.0 / total_routed)

    most = pl.ds(0, (n_ctx - 1) * HEAD)
    arrived(gv_ref.at[:, most], CH_GV)
    arrived(gk_ref.at[:, most], CH_GK)
    arrived(gq_ref.at[:, most], CH_GQ)
    for copy in own:
        copy.wait()
    for ref, channel in (
        (v_all, CH_K),
        (v_all, CH_Q),
        (v_all, CH_V),
        (d_all, CH_D),
        (live_all, CH_LIVE),
        (delta_all, CH_DELTA),
        (sum_all, CH_SUM),
        (gq_send, CH_GQ),
        (gk_send, CH_GK),
        (gv_send, CH_GV),
    ):
        sent(ref.at[few], channel)
    if n_z > 1:
        sent(w_all.at[pl.ds(0, n_z - 1)], CH_W_Z)
        sent(term_z.at[pl.ds(0, n_z - 1)], CH_TERM_Z)
    if n_y > 1:
        sent(w_all.at[pl.ds(0, (n_y - 1) * n_z)], CH_W_Y)
        sent(term_y.at[pl.ds(0, n_y - 1)], CH_TERM_Y)


def widen(gq_ref, gk_ref, gv_ref, rg_ref, q_out, k_out, v_out, r_out):
    q_out[...] = gq_ref[...].astype(F32)
    k_out[...] = gk_ref[...].astype(F32)
    v_out[...] = gv_ref[...].astype(F32)
    r_out[...] = rg_ref[0]


def body(route_pos, x_routed, w_router, queries, keys, values, d_gated):
    n_ctx = lax.axis_size("ctx")
    n_dp = lax.axis_size("dp")
    n_z = 4 if n_dp >= 16 else min(2, n_dp)
    n_y = n_dp // n_z
    rows, width = queries.shape[1:]
    routed = n_ctx * rows // 2
    blocks = routed // BLOCK
    chunk = w_router.shape[0]
    vmem = pl.BlockSpec(memory_space=pltpu.VMEM)
    hbm = pl.BlockSpec(memory_space=pltpu.HBM)
    heads = pltpu.VMEM((n_ctx, rows, HEAD), BF16)
    small = pltpu.VMEM((n_ctx, 1, rows), F32)
    compact = pltpu.VMEM((routed, HEAD), BF16)
    square = pltpu.VMEM((routed, routed), BF16)
    out = jax.ShapeDtypeStruct((rows, width), BF16)
    gq, gk, gv, rg = pl.pallas_call(
        functools.partial(kernel, n_ctx, n_y, n_z),
        out_shape=(out, out, out, jax.ShapeDtypeStruct((1, chunk), F32)),
        in_specs=[vmem, vmem] + [hbm] * 5,
        out_specs=(hbm, hbm, hbm, vmem),
        scratch_shapes=[
            pltpu.VMEM(x_routed.shape[1:], BF16),
            pltpu.VMEM((rows, width), F32),
            heads,
            pltpu.VMEM((n_ctx, rows, 2 * HEAD), BF16),
            heads,
            heads,
            small,
            pltpu.VMEM((1, rows), F32),
            pltpu.VMEM((n_dp, 1, chunk), BF16),
            pltpu.VMEM((n_ctx, 8, rows), F32),
            pltpu.VMEM((blocks, BLOCK, routed + BLOCK), BF16),
            pltpu.VMEM((n_ctx, rows, routed), BF16),
            pltpu.VMEM((routed, 2 * HEAD), BF16),
            pltpu.VMEM((HEAD, routed), BF16),
            compact,
            compact,
            square,
            square,
            pltpu.VMEM((routed, 2 * HEAD), BF16),
            compact,
            small,
            small,
            heads,
            heads,
            heads,
            pltpu.VMEM((n_dp, 1, chunk), F32),
            pltpu.VMEM((n_y, n_z, 1, chunk), F32),
            pltpu.VMEM((n_z, 1, chunk), F32),
            pltpu.VMEM((n_z, 1, chunk), F32),
            pltpu.VMEM((1, chunk), F32),
            pltpu.VMEM((n_ctx, 1, chunk), F32),
            pltpu.SemaphoreType.DMA((8,)),
            pltpu.SemaphoreType.DMA((CHANNELS,)),
            pltpu.SemaphoreType.DMA((CHANNELS,)),
        ],
        compiler_params=pltpu.CompilerParams(collective_id=0, has_side_effects=True, vmem_limit_bytes=60 * 1024 * 1024),
        name="routed_backward",
    )(route_pos, w_router, x_routed[0], queries[0], keys[0], values[0], d_gated[0])
    steps = 2
    tile = pl.BlockSpec((rows // steps, width), lambda i: (i, 0))
    wide = jax.ShapeDtypeStruct((rows, width), F32)
    gq, gk, gv, rg = pl.pallas_call(
        widen,
        grid=(steps,),
        out_shape=(wide, wide, wide, jax.ShapeDtypeStruct((chunk,), F32)),
        in_specs=[tile, tile, tile, pl.BlockSpec((1, chunk), lambda i: (0, 0))],
        out_specs=(tile, tile, tile, pl.BlockSpec((chunk,), lambda i: (0,))),
        name="widen",
    )(gq, gk, gv, rg)
    return (gq[None], gk[None], gv[None], rg)


def solution(mesh):
    placed = (
        P("dp", "ctx"),
        P("dp", "ctx", None),
        P("dp"),
        P("dp", "ctx", None),
        P("dp", "ctx", None),
        P("dp", "ctx", None),
        P("dp", "ctx", None),
    )
    return jax.shard_map(
        body,
        mesh=mesh,
        in_specs=placed,
        out_specs=(P("dp", "ctx", None), P("dp", "ctx", None), P("dp", "ctx", None), P("dp")),
        check_vma=False,
    )
```
